32 devices in a mesh: clip: 2 (over x), seq: 8 (over z, y), fsdp: 2 (over core).
Axes of the slice: x: 2, y: 2, z: 4, core: 2. Of those that a mesh axis runs over, the one named last changes fastest.
Arguments:
- tokens: bfloat16 [2, 16, 256, 1152], P('clip', 'seq', 'fsdp'), may hold values from -6 to 6
- condition: bfloat16 [2, 1152], P('clip'), may hold values from -6 to 6
- space_adaw: bfloat16 [1152, 6912], P('clip', ('seq', 'fsdp')), may hold values from -0.1875 to 0.1875
- space_adab: bfloat16 [6912], P('clip'), may hold values from -3 to 3
- space_qkv: bfloat16 [1152, 3456], P('clip', ('seq', 'fsdp')), may hold values from -0.1875 to 0.1875
- space_qvb: bfloat16 [2304], P('clip'), may hold values from -3 to 3
- space_proj: bfloat16 [1152, 1152], P('clip', ('seq', 'fsdp')), may hold values from -0.75 to 0.75
- space_projb: bfloat16 [1152], P('clip'), may hold values from -1.796875 to 1.796875
- space_up: bfloat16 [1152, 4608], P('clip', ('seq', 'fsdp')), may hold values from -0.1875 to 0.1875
- space_upb: bfloat16 [4608], P('clip'), may hold values from -3 to 3
- space_down: bfloat16 [4608, 1152], P('clip', ('seq', 'fsdp')), may hold values from -0.09375 to 0.09375
- space_downb: bfloat16 [1152], P('clip'), may hold values from -1.796875 to 1.796875
- time_adaw: bfloat16 [1152, 6912], P('clip', ('seq', 'fsdp')), may hold values from -0.1875 to 0.1875
- time_adab: bfloat16 [6912], P('clip'), may hold values from -3 to 3
- time_qkv: bfloat16 [1152, 3456], P('clip', ('seq', 'fsdp')), may hold values from -0.1875 to 0.1875
- time_qvb: bfloat16 [2304], P('clip'), may hold values from -3 to 3
- time_proj: bfloat16 [1152, 1152], P('clip', ('seq', 'fsdp')), may hold values from -0.375 to 0.375
- time_projb: bfloat16 [1152], P('clip'), may hold values from -1.796875 to 1.796875
- time_up: bfloat16 [1152, 4608], P('clip', ('seq', 'fsdp')), may hold values from -0.1875 to 0.1875
- time_upb: bfloat16 [4608], P('clip'), may hold values from -3 to 3
- time_down: bfloat16 [4608, 1152], P('clip', ('seq', 'fsdp')), may hold values from -0.09375 to 0.09375
- time_downb: bfloat16 [1152], P('clip'), may hold values from -1.796875 to 1.796875
- cotangent: bfloat16 [2, 16, 256, 1152], P('clip', 'seq', 'fsdp'), may hold values from -6 to 6
Outputs:
- output: bfloat16 [2, 16, 256, 1152], P('clip', 'seq', 'fsdp')
- tokens_grad: float32 [2, 16, 256, 1152], P('clip', 'seq', 'fsdp')
- condition_grad: float32 [2, 1152], P('clip')
- spacegrad_adaw: float32 [1152, 6912], P('clip', ('seq', 'fsdp'))
- spacegrad_adab: float32 [6912], P('clip')
- spacegrad_qkv: float32 [1152, 3456], P('clip', ('seq', 'fsdp'))
- spacegrad_qvb: float32 [2304], P('clip')
- spacegrad_proj: float32 [1152, 1152], P('clip', ('seq', 'fsdp'))
- spacegrad_projb: float32 [1152], P('clip')
- spacegrad_up: float32 [1152, 4608], P('clip', ('seq', 'fsdp'))
- spacegrad_upb: float32 [4608], P('clip')
- spacegrad_down: float32 [4608, 1152], P('clip', ('seq', 'fsdp'))
- spacegrad_downb: float32 [1152], P('clip')
- timegrad_adaw: float32 [1152, 6912], P('clip', ('seq', 'fsdp'))
- timegrad_adab: float32 [6912], P('clip')
- timegrad_qkv: float32 [1152, 3456], P('clip', ('seq', 'fsdp'))
- timegrad_qvb: float32 [2304], P('clip')
- timegrad_proj: float32 [1152, 1152], P('clip', ('seq', 'fsdp'))
- timegrad_projb: float32 [1152], P('clip')
- timegrad_up: float32 [1152, 4608], P('clip', ('seq', 'fsdp'))
- timegrad_upb: float32 [4608], P('clip')
- timegrad_down: float32 [4608, 1152], P('clip', ('seq', 'fsdp'))
- timegrad_downb: float32 [1152], P('clip')
The draws below stay inside these ranges and needn't reach their ends.
All inputs are finite; a program needn't handle non-finite values.
Results may differ from the reference program's by a relative error of at most 0.03.
Values may be sent and summed in bfloat16 or wider, within the bound.
No kernel may reach another device: no remote copies, remote signals or barrier semaphores. Data moves between devices by JAX's collectives and lax.ppermute only.
A program may use at most 320 MiB of HBM per device.

```python
from functools import partial
import jax
import jax.numpy as jnp
from jax import lax

D = 1152
HEAD = 72
FF = 4608
FRAMES = 16
PLACES = 256
CLIPS = 2


def block_levels(key, dims, shards, smallest, top_value):
    factor_of = 1.0
    for dim, shards_of in shards:
        steps = jax.random.uniform(jax.random.fold_in(jax.random.fold_in(key, 6), dim), (shards_of,), jnp.float32, smallest / len(shards), top_value / len(shards))
        factor_of = factor_of * jnp.repeat(jnp.exp(steps), dims[dim] // shards_of).reshape((-1,) + (1,) * (len(dims) - 1 - dim))
    return factor_of


def bell_draw(rng, dims, scale, limit, cuts=(), dtype=jnp.bfloat16):
    array = jax.random.normal(rng, dims, jnp.float32) * scale
    if len(cuts) > 0:
        array = block_levels(rng, dims, cuts, -0.22, 0.18) * array
    return jnp.clip(array, min=-limit, max=limit).astype(dtype)


def setup_inputs(seed: int = 0) -> dict:
    streams_of = jax.random.split(jax.random.key(seed), 24)
    tokens = bell_draw(streams_of[0], (CLIPS, FRAMES, PLACES, D), 1.0, 6.0, ((0, 2), (1, 8), (2, 2)))
    condition = bell_draw(streams_of[1], (CLIPS, D), 1.0, 6.0, ((0, 2),))
    space_adaw = bell_draw(streams_of[2], (D, 6 * D), D ** -0.5, 0.1875, ((0, 2), (1, 16)))
    space_adab = bell_draw(streams_of[3], (6 * D,), 0.5, 3.0, ((0, 2),))
    space_qkv = bell_draw(streams_of[4], (D, 3 * D), D ** -0.5, 0.1875, ((0, 2), (1, 16)))
    space_qvb = bell_draw(streams_of[5], (2 * D,), 0.5, 3.0, ((0, 2),))
    space_proj = bell_draw(streams_of[6], (D, D), (D // 16) ** -0.5, 0.75, ((0, 2), (1, 16)))
    space_projb = bell_draw(streams_of[7], (D,), 0.3, 1.796875, ((0, 2),))
    space_up = bell_draw(streams_of[8], (D, FF), D ** -0.5, 0.1875, ((0, 2), (1, 16)))
    space_upb = bell_draw(streams_of[9], (FF,), 0.5, 3.0, ((0, 2),))
    space_down = bell_draw(streams_of[10], (FF, D), FF ** -0.5, 0.09375, ((0, 2), (1, 16)))
    space_downb = bell_draw(streams_of[11], (D,), 0.3, 1.796875, ((0, 2),))
    time_adaw = bell_draw(streams_of[12], (D, 6 * D), D ** -0.5, 0.1875, ((0, 2), (1, 16)))
    time_adab = bell_draw(streams_of[13], (6 * D,), 0.5, 3.0, ((0, 2),))
    time_qkv = bell_draw(streams_of[14], (D, 3 * D), D ** -0.5, 0.1875, ((0, 2), (1, 16)))
    time_qvb = bell_draw(streams_of[15], (2 * D,), 0.5, 3.0, ((0, 2),))
    time_proj = bell_draw(streams_of[16], (D, D), (D // 4) ** -0.5, 0.375, ((0, 2), (1, 16)))
    time_projb = bell_draw(streams_of[17], (D,), 0.3, 1.796875, ((0, 2),))
    time_up = bell_draw(streams_of[18], (D, FF), D ** -0.5, 0.1875, ((0, 2), (1, 16)))
    time_upb = bell_draw(streams_of[19], (FF,), 0.5, 3.0, ((0, 2),))
    time_down = bell_draw(streams_of[20], (FF, D), FF ** -0.5, 0.09375, ((0, 2), (1, 16)))
    time_downb = bell_draw(streams_of[21], (D,), 0.3, 1.796875, ((0, 2),))
    cotangent = bell_draw(streams_of[22], (CLIPS, FRAMES, PLACES, D), 1.0, 6.0, ((0, 2), (1, 8), (2, 2)))
    return dict(tokens=tokens, condition=condition, space_adaw=space_adaw, space_adab=space_adab, space_qkv=space_qkv, space_qvb=space_qvb, space_proj=space_proj, space_projb=space_projb, space_up=space_up, space_upb=space_upb, space_down=space_down, space_downb=space_downb, time_adaw=time_adaw, time_adab=time_adab, time_qkv=time_qkv, time_qvb=time_qvb, time_proj=time_proj, time_projb=time_projb, time_up=time_up, time_upb=time_upb, time_down=time_down, time_downb=time_downb, cotangent=cotangent)


highest = lax.Precision.HIGHEST
norm_eps = 1e-06
space_forms = ('fqhd,fkhd->fhqk', 'fhqk,fkhd->fqhd')
time_forms = ('qphd,kphd->phqk', 'phqk,kphd->qphd')

@jax.custom_vjp
def low(v):
    return lax.optimization_barrier(v.astype(jnp.bfloat16)).astype(jnp.float32)

@jax.custom_vjp
def low_back(v):
    return v

def low_keep(v):
    return (low(v), None)

def low_pass(kept, grad):
    return (grad,)

def back_keep(v):
    return (v, None)

def back_low(kept, grad):
    return (low(grad),)
low.defvjp(low_keep, low_pass)
low_back.defvjp(back_keep, back_low)

def layer_norm(resid):
    center = resid - lax.optimization_barrier(jnp.mean(resid, axis=-1, keepdims=True))
    spread = lax.optimization_barrier(jnp.mean(center * center, axis=-1, keepdims=True))
    return center * lax.rsqrt(spread + norm_eps)

def attention(query, keys, values, forms):
    scores = low_back(jnp.einsum(forms[0], query, keys, precision=highest) * HEAD ** (-0.5))
    weights = low(jax.nn.softmax(scores, axis=-1))
    return jnp.einsum(forms[1], weights, values, precision=highest)

def clip_block(resid, modulation, weights, forms):
    qkv_w, qv_b, proj_w, proj_b, up_w, up_b, down_w, down_b = weights
    frames, places, width = resid.shape
    parts = jnp.split(modulation, 6)
    normed_in = low(layer_norm(resid) * (1.0 + parts[1]) + parts[0]).reshape(-1, width)
    bias_three = jnp.concatenate([qv_b[:width], jnp.zeros((width,), jnp.float32), qv_b[width:]])
    projected = low_back(low(jnp.dot(normed_in, qkv_w, precision=highest) + bias_three))
    head_shape = (frames, places, width // HEAD, HEAD)
    query = projected[:, :width].reshape(head_shape)
    keys = projected[:, width:2 * width].reshape(head_shape)
    values = projected[:, 2 * width:].reshape(head_shape)
    mixed = low_back(low(attention(query, keys, values, forms))).reshape(-1, width)
    proj_out = low_back(jnp.dot(mixed, proj_w, precision=highest) + proj_b).reshape(resid.shape)
    middle = resid + parts[2] * proj_out
    normed_mid = low(layer_norm(middle) * (1.0 + parts[4]) + parts[3]).reshape(-1, width)
    hidden = low_back(jnp.dot(normed_mid, up_w, precision=highest) + up_b)
    active = low(jax.nn.gelu(hidden, approximate=True))
    branch = low_back(jnp.dot(active, down_w, precision=highest) + down_b).reshape(resid.shape)
    return middle + parts[5] * branch

def run_block(resid, modulation, params, forms):
    step = jax.checkpoint(partial(clip_block, forms=forms))

    def one_clip(pair):
        return step(pair[0], pair[1], params[2:])
    return lax.map(one_clip, (resid, modulation))

def forward(tokens, condition, space_params, time_params):
    cond_act = low(jax.nn.silu(condition))
    resid = tokens
    for params, forms in ((space_params, space_forms), (time_params, time_forms)):
        modulation = low_back(jnp.dot(cond_act, params[0], precision=highest) + params[1])
        resid = run_block(resid, modulation, params, forms)
    return resid

def reference(tokens, condition, space_adaw, space_adab, space_qkv, space_qvb, space_proj, space_projb, space_up, space_upb, space_down, space_downb, time_adaw, time_adab, time_qkv, time_qvb, time_proj, time_projb, time_up, time_upb, time_down, time_downb, cotangent):
    space_params = tuple((item.astype(jnp.float32) for item in (space_adaw, space_adab, space_qkv, space_qvb, space_proj, space_projb, space_up, space_upb, space_down, space_downb)))
    time_params = tuple((item.astype(jnp.float32) for item in (time_adaw, time_adab, time_qkv, time_qvb, time_proj, time_projb, time_up, time_upb, time_down, time_downb)))
    result, pullback = jax.vjp(forward, tokens.astype(jnp.float32), condition.astype(jnp.float32), space_params, time_params)
    tokens_grad, condition_grad, space_grads, time_grads = pullback(cotangent.astype(jnp.float32))
    return (result.astype(jnp.bfloat16), tokens_grad, condition_grad, space_grads[0], space_grads[1], space_grads[2], space_grads[3], space_grads[4], space_grads[5], space_grads[6], space_grads[7], space_grads[8], space_grads[9], time_grads[0], time_grads[1], time_grads[2], time_grads[3], time_grads[4], time_grads[5], time_grads[6], time_grads[7], time_grads[8], time_grads[9])
```

```python
from functools import partial

import jax
import jax.numpy as jnp
from jax import lax
from jax.experimental import pallas as pl
from jax.experimental.pallas import tpu as pltpu
from jax.sharding import PartitionSpec as P

HEAD = 72


norm_eps = 1e-06
space_forms = ("cfqhd,cfkhd->cfhqk", "cfhqk,cfkhd->cfqhd", "cfhqk,cfqhd->cfkhd")
time_forms = ("cqphd,ckphd->cphqk", "cphqk,ckphd->cqphd", "cphqk,cqphd->ckphd")


def norm_mod(resid, shift, scale):
    center = resid - jnp.mean(resid, axis=-1, keepdims=True)
    spread = jnp.mean(center * center, axis=-1, keepdims=True)
    normed = center * lax.rsqrt(spread + norm_eps)
    return normed * (1.0 + scale[:, None, None, :]) + shift[:, None, None, :]


def gelu_tanh(value):
    return jax.nn.gelu(value, approximate=True)


def split_heads(block):
    return block.reshape(block.shape[:-1] + (block.shape[-1] // HEAD, HEAD))


def join_heads(block):
    return block.reshape(block.shape[:-2] + (block.shape[-2] * block.shape[-1],))


def weight_grad(left, right):
    return lax.dot_general(
        left, right, (((0,), (0,)), ((), ())), preferred_element_type=jnp.float32
    )


def back_dot(grad_rows, weight):
    return lax.dot_general(
        grad_rows, weight, (((1,), (1,)), ((), ())), preferred_element_type=jnp.float32
    )


def attend(query, keys, values, forms):
    scale = HEAD ** (-0.5)
    scores = jnp.einsum(forms[0], query, keys, preferred_element_type=jnp.float32) * scale
    peak = jnp.max(scores, axis=-1, keepdims=True)
    expo = jnp.exp(scores - peak)
    total = jnp.sum(expo, axis=-1, keepdims=True)
    weights = (expo / total).astype(jnp.bfloat16)
    mixed = jnp.einsum(forms[1], weights, values, preferred_element_type=jnp.float32)
    return (mixed, peak + jnp.log(total))


def attend_back(query, keys, values, normalizer, grad_out, forms):
    scale = HEAD ** (-0.5)
    scores = jnp.einsum(forms[0], query, keys, preferred_element_type=jnp.float32) * scale
    probs = jnp.exp(scores - normalizer)
    grad_probs = jnp.einsum(forms[0], grad_out, values, preferred_element_type=jnp.float32)
    center = jnp.sum(probs * grad_probs, axis=-1, keepdims=True)
    grad_scores = (probs * (grad_probs - center)).astype(jnp.bfloat16)
    grad_query = jnp.einsum(forms[1], grad_scores, keys, preferred_element_type=jnp.float32) * scale
    grad_keys = jnp.einsum(forms[2], grad_scores, query, preferred_element_type=jnp.float32) * scale
    grad_values = jnp.einsum(
        forms[2], probs.astype(jnp.bfloat16), grad_out, preferred_element_type=jnp.float32
    )
    return (grad_query, grad_keys, grad_values)


def fetch_weights(shards):
    mod_w, mod_b, qkv_w, qv_b, proj_w, proj_b, up_w, up_b, down_w, down_b = shards
    wide = (
        lax.all_gather(mod_w, ("seq", "fsdp"), axis=1, tiled=True),
        lax.all_gather(qkv_w, ("seq", "fsdp"), axis=1, tiled=True),
        lax.all_gather(proj_w, ("seq", "fsdp"), axis=1, tiled=True),
        lax.all_gather(up_w, ("seq", "fsdp"), axis=1, tiled=True),
        lax.all_gather(down_w, ("seq", "fsdp"), axis=1, tiled=True),
    )
    whole = (
        lax.all_gather(wide[0], "clip", axis=0, tiled=True),
        lax.all_gather(wide[1], "clip", axis=0, tiled=True),
        lax.all_gather(wide[2], "clip", axis=0, tiled=True),
        lax.all_gather(wide[3], "clip", axis=0, tiled=True),
        lax.all_gather(wide[4], "clip", axis=0, tiled=True),
        lax.all_gather(mod_b, "clip", axis=0, tiled=True),
        lax.all_gather(qv_b, "clip", axis=0, tiled=True),
        lax.all_gather(proj_b, "clip", axis=0, tiled=True),
        lax.all_gather(up_b, "clip", axis=0, tiled=True),
        lax.all_gather(down_b, "clip", axis=0, tiled=True),
    )
    return (
        whole[0],
        whole[5],
        whole[1],
        whole[6],
        whole[2],
        whole[7],
        whole[3],
        whole[8],
        whole[4],
        whole[9],
    )


def layer_forward(resid, cond_act, full, spatial):
    mod_w, mod_b, qkv_w, qv_b, proj_w, proj_b, up_w, up_b, down_w, down_b = full
    width = resid.shape[-1]
    modulation = jnp.dot(cond_act, mod_w, preferred_element_type=jnp.float32) + mod_b.astype(
        jnp.float32
    )
    parts = jnp.split(modulation, 6, axis=1)
    normed_in = norm_mod(resid, parts[0], parts[1]).astype(jnp.bfloat16)
    bias_three = jnp.concatenate(
        [
            qv_b[:width].astype(jnp.float32),
            jnp.zeros((width,), jnp.float32),
            qv_b[width:].astype(jnp.float32),
        ]
    )
    projected = (
        jnp.dot(normed_in.reshape(-1, width), qkv_w, preferred_element_type=jnp.float32)
        + bias_three
    )
    projected = projected.astype(jnp.bfloat16).reshape(resid.shape[:-1] + (3 * width,))
    query = projected[..., :width]
    keys = projected[..., width : 2 * width]
    values = projected[..., 2 * width :]
    if spatial:
        keys_all, values_all = (
            lax.all_gather(keys, "fsdp", axis=2, tiled=True),
            lax.all_gather(values, "fsdp", axis=2, tiled=True),
        )
        mixed, normalizer = attend(
            split_heads(query), split_heads(keys_all), split_heads(values_all), space_forms
        )
        state = (query, keys_all, values_all, normalizer)
        att_out = join_heads(mixed.astype(jnp.bfloat16))
    else:
        keys_all, values_all = (
            lax.all_gather(keys, "seq", axis=1, tiled=True),
            lax.all_gather(values, "seq", axis=1, tiled=True),
        )
        mixed, normalizer = attend(
            split_heads(query), split_heads(keys_all), split_heads(values_all), time_forms
        )
        state = (query, keys_all, values_all, normalizer)
        att_out = join_heads(mixed.astype(jnp.bfloat16))
    proj_out = (
        jnp.dot(att_out.reshape(-1, width), proj_w, preferred_element_type=jnp.float32)
        + proj_b.astype(jnp.float32)
    ).reshape(resid.shape)
    middle = resid + parts[2][:, None, None, :] * proj_out
    normed_mid = norm_mod(middle, parts[3], parts[4]).astype(jnp.bfloat16)
    hidden = jnp.dot(
        normed_mid.reshape(-1, width), up_w, preferred_element_type=jnp.float32
    ) + up_b.astype(jnp.float32)
    active = gelu_tanh(hidden).astype(jnp.bfloat16)
    branch = (
        jnp.dot(active, down_w, preferred_element_type=jnp.float32) + down_b.astype(jnp.float32)
    ).reshape(resid.shape)
    result = middle + parts[5][:, None, None, :] * branch
    kept = (
        resid,
        parts,
        normed_in,
        state,
        att_out,
        proj_out,
        middle,
        normed_mid,
        hidden,
        active,
        branch,
    )
    return (result, kept)


def layer_backward(incoming, kept, full, spatial, grad_form):
    (
        resid,
        parts,
        normed_in,
        state,
        att_out,
        proj_out,
        middle,
        normed_mid,
        hidden,
        active,
        branch,
    ) = kept
    mod_w, mod_b, qkv_w, qv_b, proj_w, proj_b, up_w, up_b, down_w, down_b = full
    width = resid.shape[-1]
    grad_gate2 = jnp.sum(incoming * branch, axis=(1, 2))
    grad_branch = (parts[5][:, None, None, :] * incoming).astype(jnp.bfloat16).reshape(-1, width)
    grad_down = grad_form(active, grad_branch)
    bias_down = jnp.sum(grad_branch, axis=0, dtype=jnp.float32)
    grad_active = back_dot(grad_branch, down_w)
    unused, gelu_back = jax.vjp(gelu_tanh, hidden)
    grad_hidden = gelu_back(grad_active)[0].astype(jnp.bfloat16)
    grad_up = grad_form(normed_mid.reshape(-1, width), grad_hidden)
    bias_up = jnp.sum(grad_hidden, axis=0, dtype=jnp.float32)
    grad_second = back_dot(grad_hidden, up_w).reshape(resid.shape)
    unused, norm_back_mid = jax.vjp(norm_mod, middle, parts[3], parts[4])
    grad_from, grad_shift2, grad_scale2 = norm_back_mid(grad_second)
    grad_middle = incoming + grad_from
    grad_gate1 = jnp.sum(grad_middle * proj_out, axis=(1, 2))
    grad_proj = (parts[2][:, None, None, :] * grad_middle).astype(jnp.bfloat16).reshape(-1, width)
    grad_projw = grad_form(att_out.reshape(-1, width), grad_proj)
    bias_proj = jnp.sum(grad_proj, axis=0, dtype=jnp.float32)
    grad_att = back_dot(grad_proj, proj_w).astype(jnp.bfloat16).reshape(resid.shape)
    query_s, keys_s, values_s, normalizer = state
    if spatial:
        query_terms, key_terms, value_terms = attend_back(
            split_heads(query_s),
            split_heads(keys_s),
            split_heads(values_s),
            normalizer,
            split_heads(grad_att),
            space_forms,
        )
        grad_keys, grad_values = (
            lax.psum_scatter(
                join_heads(key_terms).astype(jnp.bfloat16), "fsdp", scatter_dimension=2, tiled=True
            ).astype(jnp.float32),
            lax.psum_scatter(
                join_heads(value_terms).astype(jnp.bfloat16),
                "fsdp",
                scatter_dimension=2,
                tiled=True,
            ).astype(jnp.float32),
        )
        grad_query = join_heads(query_terms)
    else:
        query_terms, key_terms, value_terms = attend_back(
            split_heads(query_s),
            split_heads(keys_s),
            split_heads(values_s),
            normalizer,
            split_heads(grad_att),
            time_forms,
        )
        grad_keys, grad_values = (
            lax.psum_scatter(
                join_heads(key_terms).astype(jnp.bfloat16), "seq", scatter_dimension=1, tiled=True
            ).astype(jnp.float32),
            lax.psum_scatter(
                join_heads(value_terms).astype(jnp.bfloat16), "seq", scatter_dimension=1, tiled=True
            ).astype(jnp.float32),
        )
        grad_query = join_heads(query_terms)
    grad_three = jnp.concatenate(
        [
            grad_query.astype(jnp.bfloat16),
            grad_keys.astype(jnp.bfloat16),
            grad_values.astype(jnp.bfloat16),
        ],
        axis=3,
    ).reshape(-1, 3 * width)
    grad_qkvw = grad_form(normed_in.reshape(-1, width), grad_three)
    bias_qv = jnp.concatenate(
        [
            jnp.sum(grad_three[:, :width], axis=0, dtype=jnp.float32),
            jnp.sum(grad_three[:, 2 * width :], axis=0, dtype=jnp.float32),
        ]
    )
    grad_first = back_dot(grad_three, qkv_w).reshape(resid.shape)
    unused, norm_back_in = jax.vjp(norm_mod, resid, parts[0], parts[1])
    grad_from_in, grad_shift1, grad_scale1 = norm_back_in(grad_first)
    grad_resid = grad_middle + grad_from_in
    grad_modulation = jnp.concatenate(
        [grad_shift1, grad_scale1, grad_gate1, grad_shift2, grad_scale2, grad_gate2], axis=1
    )
    return (
        grad_resid,
        grad_modulation,
        (grad_qkvw, grad_projw, grad_up, grad_down),
        (bias_qv, bias_proj, bias_up, bias_down),
    )


def local(
    tokens,
    condition,
    space_adaw,
    space_adab,
    space_qkv,
    space_qvb,
    space_proj,
    space_projb,
    space_up,
    space_upb,
    space_down,
    space_downb,
    time_adaw,
    time_adab,
    time_qkv,
    time_qvb,
    time_proj,
    time_projb,
    time_up,
    time_upb,
    time_down,
    time_downb,
    cotangent,
):
    cond_in = condition.astype(jnp.float32)
    cond_act = jax.nn.silu(cond_in).astype(jnp.bfloat16)
    layers = (
        (
            space_adaw,
            space_adab,
            space_qkv,
            space_qvb,
            space_proj,
            space_projb,
            space_up,
            space_upb,
            space_down,
            space_downb,
        ),
        (
            time_adaw,
            time_adab,
            time_qkv,
            time_qvb,
            time_proj,
            time_projb,
            time_up,
            time_upb,
            time_down,
            time_downb,
        ),
    )
    resid = tokens.astype(jnp.float32)
    gathered = []
    saved = []
    for index in range(2):
        full = fetch_weights(layers[index])
        resid, kept = layer_forward(resid, cond_act, full, index == 0)
        gathered.append(full)
        saved.append(kept)
    output = resid.astype(jnp.bfloat16)
    incoming = cotangent.astype(jnp.float32)
    grad_act = jnp.zeros(cond_in.shape, jnp.float32)
    results = [None, None]
    for index in (1, 0):
        full = gathered[index]
        incoming, grad_mod, weight_terms, bias_terms = layer_backward(
            incoming, saved[index], full, index == 0, weight_grad
        )
        summed = (
            lax.psum(grad_mod.astype(jnp.bfloat16), ("seq", "fsdp")).astype(jnp.float32),
            lax.psum(bias_terms[0].astype(jnp.bfloat16), ("seq", "fsdp")).astype(jnp.float32),
            lax.psum(bias_terms[1].astype(jnp.bfloat16), ("seq", "fsdp")).astype(jnp.float32),
            lax.psum(bias_terms[2].astype(jnp.bfloat16), ("seq", "fsdp")).astype(jnp.float32),
            lax.psum(bias_terms[3].astype(jnp.bfloat16), ("seq", "fsdp")).astype(jnp.float32),
        )
        mod_low = summed[0].astype(jnp.bfloat16)
        grad_act = grad_act + back_dot(mod_low, full[0])
        columns = layers[index][0].shape[1]
        mod_cols = lax.dynamic_slice_in_dim(
            mod_low, lax.axis_index(("seq", "fsdp")) * columns, columns, 1
        )
        ada_cols = weight_grad(cond_act, mod_cols)
        ada_bias = jnp.sum(mod_low, axis=0, dtype=jnp.float32)
        row_parts = (
            lax.psum_scatter(
                ada_cols.astype(jnp.bfloat16), "clip", scatter_dimension=0, tiled=True
            ).astype(jnp.float32),
            lax.psum_scatter(
                weight_terms[0].astype(jnp.bfloat16), "clip", scatter_dimension=0, tiled=True
            ).astype(jnp.float32),
            lax.psum_scatter(
                weight_terms[1].astype(jnp.bfloat16), "clip", scatter_dimension=0, tiled=True
            ).astype(jnp.float32),
            lax.psum_scatter(
                weight_terms[2].astype(jnp.bfloat16), "clip", scatter_dimension=0, tiled=True
            ).astype(jnp.float32),
            lax.psum_scatter(
                weight_terms[3].astype(jnp.bfloat16), "clip", scatter_dimension=0, tiled=True
            ).astype(jnp.float32),
            lax.psum_scatter(
                ada_bias.astype(jnp.bfloat16), "clip", scatter_dimension=0, tiled=True
            ).astype(jnp.float32),
            lax.psum_scatter(
                summed[1].astype(jnp.bfloat16), "clip", scatter_dimension=0, tiled=True
            ).astype(jnp.float32),
            lax.psum_scatter(
                summed[2].astype(jnp.bfloat16), "clip", scatter_dimension=0, tiled=True
            ).astype(jnp.float32),
            lax.psum_scatter(
                summed[3].astype(jnp.bfloat16), "clip", scatter_dimension=0, tiled=True
            ).astype(jnp.float32),
            lax.psum_scatter(
                summed[4].astype(jnp.bfloat16), "clip", scatter_dimension=0, tiled=True
            ).astype(jnp.float32),
        )
        col_parts = (
            lax.psum_scatter(
                row_parts[1].astype(jnp.bfloat16), ("seq", "fsdp"), scatter_dimension=1, tiled=True
            ).astype(jnp.float32),
            lax.psum_scatter(
                row_parts[2].astype(jnp.bfloat16), ("seq", "fsdp"), scatter_dimension=1, tiled=True
            ).astype(jnp.float32),
            lax.psum_scatter(
                row_parts[3].astype(jnp.bfloat16), ("seq", "fsdp"), scatter_dimension=1, tiled=True
            ).astype(jnp.float32),
            lax.psum_scatter(
                row_parts[4].astype(jnp.bfloat16), ("seq", "fsdp"), scatter_dimension=1, tiled=True
            ).astype(jnp.float32),
        )
        results[index] = (
            row_parts[0],
            row_parts[5],
            col_parts[0],
            row_parts[6],
            col_parts[1],
            row_parts[7],
            col_parts[2],
            row_parts[8],
            col_parts[3],
            row_parts[9],
        )
    unused, silu_back = jax.vjp(jax.nn.silu, cond_in)
    condition_grad = silu_back(grad_act)[0]
    return (output, incoming, condition_grad) + results[0] + results[1]


SWAP = [(0, 1), (1, 0)]
BF = jnp.bfloat16
F32 = jnp.float32


def swap_core(value):
    return lax.ppermute(value, "fsdp", SWAP)


def swap_clip(value):
    return lax.ppermute(value, "clip", SWAP)


class Ring:
    def __init__(self, size):
        half = size // 2
        self.size = size
        order = [2 * row for row in range(half)] + [2 * row + 1 for row in reversed(range(half))]
        self.ahead = [(order[at], order[(at + 1) % size]) for at in range(size)]
        self.behind = [(to, frm) for frm, to in self.ahead]
        here = lax.axis_index("seq")
        row, column = here // 2, here % 2
        self.position = jnp.where(column == 0, row, size - 1 - row)

    def chip(self, offset):
        at = (self.position + offset + self.size) % self.size
        return jnp.where(at < self.size // 2, 2 * at, 2 * (self.size - 1 - at) + 1)

    def send_ahead(self, value):
        return lax.ppermute(value, "seq", self.ahead)

    def send_behind(self, value):
        return lax.ppermute(value, "seq", self.behind)


def half_rows(rows):
    return (rows // 2 + 7) // 8 * 8


def ring_gather(ring, pieces, after=None):
    if after is not None:
        *pieces, _ = lax.optimization_barrier((*pieces, after))
    steps = ring.size // 2
    stores = []
    for piece in pieces:
        store = jnp.zeros((ring.size,) + piece.shape, piece.dtype)
        stores.append(lax.dynamic_update_index_in_dim(store, piece, ring.chip(0), 0))
    front = list(pieces)
    back = list(pieces)
    marker = None
    for step in range(1, steps + 1):
        last = step == steps
        for at in range(len(pieces)):
            cut = half_rows(pieces[at].shape[0])
            if last:
                marker = front[at] if at == 0 else marker
                low_part = ring.send_ahead(front[at][:cut])
                high_part = ring.send_behind(back[at][cut:])
                joined = jnp.concatenate([low_part, high_part], axis=0)
                stores[at] = lax.dynamic_update_index_in_dim(
                    stores[at], joined, ring.chip(steps), 0
                )
            else:
                front[at] = ring.send_ahead(front[at])
                back[at] = ring.send_behind(back[at])
                stores[at] = lax.dynamic_update_index_in_dim(
                    stores[at], front[at], ring.chip(-step), 0
                )
                stores[at] = lax.dynamic_update_index_in_dim(
                    stores[at], back[at], ring.chip(step), 0
                )
    whole = [store.reshape((-1, store.shape[-1])) for store in stores]
    return whole, marker


def ring_scatter(ring, sums):
    steps = ring.size // 2
    results = []
    for total in sums:
        parts = total.reshape((ring.size, -1, total.shape[-1]))
        cut = half_rows(parts.shape[1])

        def own(offset):
            return lax.dynamic_index_in_dim(parts, ring.chip(offset), 0, keepdims=False)

        far = own(steps)
        front = ring.send_ahead(far[:cut])
        back = ring.send_behind(far[cut:])
        for step in range(steps - 1, 0, -1):
            mine_front = own(step).astype(F32)
            mine_back = own(-step).astype(F32)
            if step == steps - 1:
                front = jnp.concatenate(
                    [mine_front[:cut] + front.astype(F32), mine_front[cut:]], axis=0
                )
                back = jnp.concatenate(
                    [mine_back[:cut], mine_back[cut:] + back.astype(F32)], axis=0
                )
            else:
                front = mine_front + front.astype(F32)
                back = mine_back + back.astype(F32)
            front = ring.send_ahead(front.astype(BF))
            back = ring.send_behind(back.astype(BF))
        results.append(own(0).astype(F32) + front.astype(F32) + back.astype(F32))
    return results


def pick(flag, when_zero, when_one):
    return jnp.where(flag == 0, when_zero, when_one)


def order_two(flag, mine, other, axis):
    return pick(
        flag,
        jnp.concatenate([mine, other], axis=axis),
        jnp.concatenate([other, mine], axis=axis),
    )


def stack_two(flag, mine, other, axis):
    return pick(flag, jnp.stack([mine, other], axis), jnp.stack([other, mine], axis))


def prepare_attention(qkv_w, proj_w, clip, core):
    turned = qkv_w.T
    mid = swap_core(turned[HEAD : 2 * HEAD])
    ends = jnp.concatenate([turned[:HEAD], turned[2 * HEAD :]], axis=0)
    turned = pick(
        core, jnp.concatenate([ends, mid], axis=0), jnp.concatenate([mid, ends], axis=0)
    )
    qkv_piece = order_two(clip, turned, swap_clip(turned), 1)
    rows, columns = proj_w.shape
    by_head = proj_w.reshape(rows // HEAD // 2, 2, HEAD, columns)
    keep = pick(core, by_head[:, 0], by_head[:, 1])
    give = pick(core, by_head[:, 1], by_head[:, 0])
    joined = order_two(core, keep, swap_core(give), 2).reshape(rows // 2, 2 * columns)
    proj_piece = order_two(clip, joined, swap_clip(joined), 0).T
    return (qkv_piece, proj_piece)


def prepare_mlp(up_w, down_w, clip, core):
    turned = up_w.T
    half = turned.shape[0] // 2
    keep = pick(clip, turned[:half], turned[half:])
    give = pick(clip, turned[half:], turned[:half])
    up_piece = order_two(clip, keep, swap_clip(give), 1)
    columns = down_w.shape[1]
    cells = down_w.reshape(-1, 2, 2, half, columns)
    keep = pick(clip, cells[:, :, 0], cells[:, :, 1])
    give = pick(clip, cells[:, :, 1], cells[:, :, 0])
    cells = order_two(clip, keep, swap_clip(give), 0)
    keep = pick(core, cells[:, 0], cells[:, 1])
    give = pick(core, cells[:, 1], cells[:, 0])
    joined = order_two(core, keep, swap_core(give), 2)
    down_piece = joined.reshape(-1, 2 * columns).T
    return (up_piece, down_piece)


def finish_qkv(summed, clip, core):
    half = summed.shape[1] // 2
    mine = pick(clip, summed[:, :half], summed[:, half:])
    give = pick(clip, summed[:, half:], summed[:, :half]).astype(BF)
    mine = mine + swap_clip(give).astype(F32)
    first, second, third = mine[:HEAD], mine[HEAD : 2 * HEAD], mine[2 * HEAD :]
    mid = swap_core(pick(core, third, first))
    return jnp.concatenate([pick(core, first, second), mid, pick(core, second, third)], axis=0).T


def finish_proj(summed, clip, core):
    half = summed.shape[1] // 2
    mine = pick(clip, summed[:, :half], summed[:, half:])
    give = pick(clip, summed[:, half:], summed[:, :half]).astype(BF)
    mine = mine + swap_clip(give).astype(F32)
    columns = mine.shape[0] // 2
    keep = pick(core, mine[:columns], mine[columns:]).T.reshape(-1, HEAD, columns)
    give = pick(core, mine[columns:], mine[:columns]).T.reshape(-1, HEAD, columns)
    return stack_two(core, keep, swap_core(give), 1).reshape(-1, columns)


def finish_up(summed, clip, core):
    half = summed.shape[1] // 2
    keep = pick(clip, summed[:, :half], summed[:, half:])
    give = pick(clip, summed[:, half:], summed[:, :half]).astype(BF)
    return order_two(clip, keep, swap_clip(give).astype(F32), 0).T


def finish_down(summed, clip, core, ring, cell):
    columns = summed.shape[0] // 2
    keep = pick(core, summed[:columns], summed[columns:]).T.reshape(ring.size, cell, columns)
    give = pick(core, summed[columns:], summed[:columns]).astype(BF).T
    other = swap_core(give).astype(F32).reshape(ring.size, cell, columns)
    both = stack_two(core, keep, other, 1)
    half = ring.size // 2
    keep = pick(clip, both[:half], both[half:])
    give = pick(clip, both[half:], both[:half]).astype(BF)
    return stack_two(clip, keep, swap_clip(give).astype(F32), 2).reshape(-1, columns)


def softmax_rows(query, keys, masked, group):
    scores = lax.dot_general(
        query, keys, (((1,), (1,)), ((), ())), preferred_element_type=F32
    ) * HEAD ** (-0.5)
    if masked:
        rows = lax.broadcasted_iota(jnp.int32, scores.shape, 0)
        cols = lax.broadcasted_iota(jnp.int32, scores.shape, 1)
        scores = jnp.where(rows % group == cols % group, scores, -1e30)
    peak = jnp.max(scores, axis=-1, keepdims=True)
    expo = jnp.exp(scores - peak)
    return expo / jnp.sum(expo, axis=-1, keepdims=True)


def load_rows(ref):
    value = ref[...]
    return value.reshape(-1, value.shape[-1])


def attention_kernel(qkv_ref, out_ref, *, masked, group):
    block = load_rows(qkv_ref)
    width = block.shape[1] // 3
    outs = []
    for at in range(0, width, HEAD):
        probs = softmax_rows(
            block[:, at : at + HEAD], block[:, width + at : width + at + HEAD], masked, group
        ).astype(BF)
        outs.append(
            jnp.dot(
                probs,
                block[:, 2 * width + at : 2 * width + at + HEAD],
                preferred_element_type=F32,
            ).astype(BF)
        )
    out_ref[...] = jnp.concatenate(outs, axis=1).reshape(out_ref.shape)


def attention_back_kernel(qkv_ref, grad_ref, out_ref, *, masked, group):
    block = load_rows(qkv_ref)
    grads = load_rows(grad_ref)
    width = block.shape[1] // 3
    scale = HEAD ** (-0.5)
    grad_q, grad_k, grad_v = [], [], []
    for at in range(0, width, HEAD):
        query = block[:, at : at + HEAD]
        keys = block[:, width + at : width + at + HEAD]
        values = block[:, 2 * width + at : 2 * width + at + HEAD]
        grad = grads[:, at : at + HEAD]
        probs = softmax_rows(query, keys, masked, group)
        grad_probs = lax.dot_general(
            grad, values, (((1,), (1,)), ((), ())), preferred_element_type=F32
        )
        center = jnp.sum(probs * grad_probs, axis=-1, keepdims=True)
        grad_scores = (probs * (grad_probs - center)).astype(BF)
        grad_q.append(
            (jnp.dot(grad_scores, keys, preferred_element_type=F32) * scale).astype(BF)
        )
        grad_k.append((weight_grad(grad_scores, query) * scale).astype(BF))
        grad_v.append(weight_grad(probs.astype(BF), grad).astype(BF))
    out_ref[...] = jnp.concatenate(grad_q + grad_k + grad_v, axis=1).reshape(out_ref.shape)


def group_spec(spatial, frames, places, width):
    if spatial:
        return pl.BlockSpec((2, 1, places, width), lambda at: (0, at, 0, 0))
    return pl.BlockSpec((1, 1, frames * places, width), lambda at: (at, 0, 0, 0))


def group_shape(spatial, frames, places, width):
    if spatial:
        return (2, frames, places, width)
    return (2, 1, frames * places, width)


def attention_call(body, inputs, out_width, spatial, frames, places, group, flops):
    steps = frames if spatial else 2
    specs = [group_spec(spatial, frames, places, item.shape[-1]) for item in inputs]
    shaped = [
        item.reshape(group_shape(spatial, frames, places, item.shape[-1])) for item in inputs
    ]
    tokens = inputs[0].shape[0]
    out = pl.pallas_call(
        partial(body, masked=not spatial, group=group),
        grid=(steps,),
        in_specs=specs,
        out_specs=group_spec(spatial, frames, places, out_width),
        out_shape=jax.ShapeDtypeStruct(group_shape(spatial, frames, places, out_width), BF),
        cost_estimate=pl.CostEstimate(
            flops=flops, bytes_accessed=tokens * 2 * 4 * out_width, transcendentals=tokens * 2048
        ),
    )(*shaped)
    return out.reshape(tokens, out_width)


def normalize(value):
    center = value - jnp.mean(value, axis=-1, keepdims=True)
    spread = jnp.mean(center * center, axis=-1, keepdims=True)
    rate = lax.rsqrt(spread + norm_eps)
    return (center * rate, rate)


def norm_back(grad, normed, rate, scale):
    grad_shift = jnp.sum(grad, axis=0)
    grad_scale = jnp.sum(grad * normed, axis=0)
    inner = grad * (1.0 + scale)
    grad_in = rate * (
        inner
        - jnp.mean(inner, axis=-1, keepdims=True)
        - normed * jnp.mean(inner * normed, axis=-1, keepdims=True)
    )
    return (grad_in, grad_shift, grad_scale)


def nt_dot(rows, weight):
    return lax.dot_general(
        rows, weight, (((1,), (1,)), ((), ())), preferred_element_type=F32
    )


def nn_dot(rows, weight):
    return jnp.dot(rows, weight, preferred_element_type=F32)


def reduce_core(partial_sum):
    half = partial_sum.shape[0] // 2
    return partial_sum[:half] + swap_core(partial_sum[half:].astype(BF)).astype(F32)


def reduce_four(near, far):
    crossing = reduce_core(far).astype(BF)
    return reduce_core(near) + swap_clip(crossing).astype(F32)


def gather_four(mine):
    across = swap_clip(mine)
    near = jnp.concatenate([mine, swap_core(mine)], axis=0)
    far = jnp.concatenate([across, swap_core(across)], axis=0)
    return (near, far)


def gelu_both(hidden):
    rate = 0.7978845608028654
    bend = 0.044715
    square = hidden * hidden
    tanh = jnp.tanh(rate * hidden * (1.0 + bend * square))
    value = 0.5 * hidden * (1.0 + tanh)
    slope = 0.5 * (1.0 + tanh) + 0.5 * hidden * (1.0 - tanh * tanh) * rate * (
        1.0 + 3.0 * bend * square
    )
    return (value.astype(BF), slope.astype(BF))


def block_forward(resid, parts, attn_w, mlp_w, biases, spatial, frames, places, group):
    qkv_t, proj_t = attn_w
    up_t, down_t = mlp_w
    bias_three, proj_b, up_b, down_b = biases
    normed1, rate1 = normalize(resid)
    first = (normed1 * (1.0 + parts[1]) + parts[0]).astype(BF)
    first_all = jnp.concatenate([first, swap_core(first)], axis=0)
    qkv = (nt_dot(first_all, qkv_t) + bias_three).astype(BF)
    width = qkv.shape[1] // 3
    mixed = attention_call(
        attention_kernel, (qkv,), width, spatial, frames, places, group, 4 * 512 * 256 * width
    )
    attended = reduce_core(nt_dot(mixed, proj_t)) + proj_b
    middle = resid + parts[2] * attended
    normed2, rate2 = normalize(middle)
    second = (normed2 * (1.0 + parts[4]) + parts[3]).astype(BF)
    seconds = gather_four(second)
    actives, slopes, branches = [], [], []
    for rows in seconds:
        active, slope = gelu_both(nt_dot(rows, up_t) + up_b)
        actives.append(active)
        slopes.append(slope)
        branches.append(nt_dot(active, down_t))
    branch = reduce_four(branches[0], branches[1]) + down_b
    result = middle + parts[5] * branch
    kept = (resid, middle, first_all, qkv, mixed, attended, seconds, actives, slopes, branch)
    return (result, kept)


def block_backward(incoming, kept, parts, attn_w, mlp_w, ring, spatial, frames, places, group):
    resid, middle, first_all, qkv, mixed, attended, seconds, actives, slopes, branch = kept
    qkv_t, proj_t = attn_w
    up_t, down_t = mlp_w
    grad_gate2 = jnp.sum(incoming * branch, axis=0)
    grad_branch = (parts[5] * incoming).astype(BF)
    bias_down = jnp.sum(grad_branch, axis=0, dtype=F32)
    branches = gather_four(grad_branch)
    seconds_grad = []
    hiddens = []
    for rows, slope in zip(branches, slopes):
        grad_hidden = (nn_dot(rows, down_t) * slope.astype(F32)).astype(BF)
        hiddens.append(grad_hidden)
        seconds_grad.append(nn_dot(grad_hidden, up_t))
    bias_up = sum(jnp.sum(item, axis=0, dtype=F32) for item in hiddens)
    grad_down = sum(weight_grad(rows, act) for rows, act in zip(branches, actives)).astype(BF)
    grad_up = sum(weight_grad(item, rows) for item, rows in zip(hiddens, seconds)).astype(BF)
    grad_second = reduce_four(seconds_grad[0], seconds_grad[1])
    normed2, rate2 = normalize(middle)
    grad_from, grad_shift2, grad_scale2 = norm_back(grad_second, normed2, rate2, parts[4])
    grad_middle = incoming + grad_from
    grad_gate1 = jnp.sum(grad_middle * attended, axis=0)
    grad_att = (parts[2] * grad_middle).astype(BF)
    bias_proj = jnp.sum(grad_att, axis=0, dtype=F32)
    grad_att_all = jnp.concatenate([grad_att, swap_core(grad_att)], axis=0)
    grad_mixed = nn_dot(grad_att_all, proj_t).astype(BF)
    grad_proj = weight_grad(grad_att_all, mixed).astype(BF)
    grad_three = attention_call(
        attention_back_kernel,
        (qkv, grad_mixed),
        qkv.shape[1],
        spatial,
        frames,
        places,
        group,
        10 * 512 * 256 * mixed.shape[1],
    )
    grad_first = reduce_core(nn_dot(grad_three, qkv_t))
    grad_qkv = weight_grad(grad_three, first_all).astype(BF)
    column_sums = jnp.sum(grad_three, axis=0, dtype=F32)
    normed1, rate1 = normalize(resid)
    grad_in, grad_shift1, grad_scale1 = norm_back(grad_first, normed1, rate1, parts[1])
    grad_resid = grad_middle + grad_in
    grad_mod = jnp.concatenate(
        [grad_shift1, grad_scale1, grad_gate1, grad_shift2, grad_scale2, grad_gate2]
    )
    scattered = ring_scatter(ring, (grad_up, grad_down)) + ring_scatter(
        ring, (grad_proj, grad_qkv)
    )
    return (grad_resid, grad_mod, scattered, (bias_down, bias_proj, bias_up, column_sums))


def to_places(rows, ring, frames, places):
    cells = rows.reshape(frames, ring.size, places // ring.size, -1)
    moved = lax.all_to_all(cells, "seq", split_axis=1, concat_axis=0, tiled=True)
    return moved.reshape(frames * places, -1)


def to_frames(rows, ring, frames, places):
    cells = rows.reshape(ring.size * frames, 1, places // ring.size, -1)
    moved = lax.all_to_all(cells, "seq", split_axis=0, concat_axis=1, tiled=True)
    return moved.reshape(frames * places, -1)


def ringed(
    ring_size,
    tokens,
    condition,
    *rest,
):
    weights, cotangent = rest[:-1], rest[-1]
    layers = (weights[:10], weights[10:])
    clip = lax.axis_index("clip")
    core = lax.axis_index("fsdp")
    seat = lax.axis_index("seq")
    ring = Ring(ring_size)
    frames, places, width = tokens.shape[1:]
    group = places // ring_size
    cell = layers[0][6].shape[1] // 2

    attn_pieces = [prepare_attention(layer[2], layer[4], clip, core) for layer in layers]
    mlp_pieces = [prepare_mlp(layer[6], layer[8], clip, core) for layer in layers]
    attn_w, mlp_w = [None, None], [None, None]
    marker = None
    for index in range(2):
        attn_w[index], marker = ring_gather(ring, attn_pieces[index], marker)
        mlp_w[index], marker = ring_gather(ring, mlp_pieces[index], marker)

    packed = jnp.concatenate(
        [layer[at] for layer in layers for at in (1, 3, 5, 7, 9)]
    ).reshape(1, -1)
    both = order_two(clip, packed, swap_clip(packed), 0).astype(F32)
    vectors = []
    start = 0
    for layer in layers:
        row = []
        for at in (1, 3, 5, 7, 9):
            size = layer[at].shape[0]
            row.append(both[:, start : start + size].reshape(-1))
            start += size
        vectors.append(row)

    cond_in = condition.astype(F32)
    cond_act = jax.nn.silu(cond_in).astype(BF)
    acts = order_two(clip, cond_act, swap_clip(cond_act), 0)
    half = width // 2
    acts_half = pick(clip, acts[:, :half], acts[:, half:])
    mod_parts = jnp.stack([nn_dot(acts_half, layer[0]) for layer in layers], axis=1)
    mine = pick(clip, mod_parts[0], mod_parts[1])
    give = pick(clip, mod_parts[1], mod_parts[0])
    mod_cols = mine + swap_clip(give)
    columns = mod_cols.shape[1]
    mods = lax.all_gather(mod_cols, ("seq", "fsdp"), axis=0)
    mods = jnp.swapaxes(mods, 0, 1).reshape(2, 6 * width)

    parts, biases = [], []
    for index in range(2):
        adab, qvb, projb, upb, downb = vectors[index]
        parts.append(jnp.split(mods[index] + adab, 6))
        by_parity = qvb.reshape(2, -1, 2, HEAD)
        mine_qv = pick(core, by_parity[:, :, 0], by_parity[:, :, 1]).reshape(2, -1)
        three = jnp.concatenate([mine_qv[0], jnp.zeros_like(mine_qv[0]), mine_qv[1]])
        cells = upb.reshape(ring_size, 2, 2, cell)
        by_core = pick(core, cells[:, 0], cells[:, 1])
        mine_up = pick(clip, by_core[:, 0], by_core[:, 1]).reshape(-1)
        biases.append((three, projb, mine_up, downb))

    resid = tokens.reshape(-1, width).astype(F32)
    resid, kept_space = block_forward(
        resid, parts[0], attn_w[0], mlp_w[0], biases[0], True, frames, places, group
    )
    resid = to_places(resid.astype(BF), ring, frames, places).astype(F32)
    resid, kept_time = block_forward(
        resid, parts[1], attn_w[1], mlp_w[1], biases[1], False, frames, places, group
    )
    output = to_frames(resid.astype(BF), ring, frames, places).reshape(tokens.shape)

    incoming = to_places(cotangent.reshape(-1, width), ring, frames, places).astype(F32)
    results = [None, None]
    grad_acts = jnp.zeros((2, half), F32)
    kept = (kept_space, kept_time)
    for index in (1, 0):
        incoming, grad_mod, scattered, sums = block_backward(
            incoming,
            kept[index],
            parts[index],
            attn_w[index],
            mlp_w[index],
            ring,
            index == 0,
            frames,
            places,
            group,
        )
        if index == 1:
            incoming = to_frames(incoming.astype(BF), ring, frames, places).astype(F32)
        bias_down, bias_proj, bias_up, column_sums = sums
        zero = jnp.zeros_like(grad_mod)
        mod_slots = stack_two(clip, grad_mod, zero, 0).reshape(-1)
        up_cells = bias_up.reshape(ring_size, cell)
        up_slots = stack_two(clip, up_cells, jnp.zeros_like(up_cells), 1)
        up_slots = stack_two(core, up_slots, jnp.zeros_like(up_slots), 1).reshape(-1)
        third = column_sums.shape[0] // 3
        qv = jnp.stack([column_sums[:third], column_sums[2 * third :]]).reshape(2, -1, HEAD)
        qv_slots = stack_two(core, qv, jnp.zeros_like(qv), 2).reshape(-1)
        vector = jnp.concatenate([mod_slots, bias_down, bias_proj, up_slots, qv_slots])
        vector = lax.psum(vector, ("clip", "seq", "fsdp"))
        sizes = [item.shape[0] for item in (mod_slots, bias_down, bias_proj, up_slots, qv_slots)]
        pieces = []
        start = 0
        for size in sizes:
            pieces.append(vector[start : start + size])
            start += size
        mod_low = pieces[0].reshape(2, -1).astype(BF)
        mod_cols = lax.dynamic_slice_in_dim(mod_low, (seat * 2 + core) * columns, columns, 1)
        grad_acts = grad_acts + back_dot(mod_cols, layers[index][0])
        ada_grad = weight_grad(acts_half, mod_cols)
        ada_bias = jnp.sum(mod_low.astype(F32), axis=0)

        def own_half(value):
            rows = value.reshape(2, -1)
            return pick(clip, rows[0], rows[1])

        results[index] = (
            ada_grad,
            own_half(ada_bias),
            finish_qkv(scattered[3], clip, core),
            own_half(pieces[4]),
            finish_proj(scattered[2], clip, core),
            own_half(pieces[2]),
            finish_up(scattered[0], clip, core),
            own_half(pieces[3]),
            finish_down(scattered[1], clip, core, ring, cell),
            own_half(pieces[1]),
        )
    tokens_grad = incoming.reshape(tokens.shape)
    slots = stack_two(clip, grad_acts, jnp.zeros_like(grad_acts), 1).reshape(2, -1)
    total = lax.psum(slots, ("clip", "seq", "fsdp"))
    grad_act = pick(clip, total[0], total[1]).reshape(cond_in.shape)
    unused, silu_back = jax.vjp(jax.nn.silu, cond_in)
    condition_grad = silu_back(grad_act)[0]
    return (output, tokens_grad, condition_grad) + results[0] + results[1]


def solution(mesh):
    in_specs = (
        P("clip", "seq", "fsdp", None),
        P("clip", None),
        P("clip", ("seq", "fsdp")),
        P("clip"),
        P("clip", ("seq", "fsdp")),
        P("clip"),
        P("clip", ("seq", "fsdp")),
        P("clip"),
        P("clip", ("seq", "fsdp")),
        P("clip"),
        P("clip", ("seq", "fsdp")),
        P("clip"),
        P("clip", ("seq", "fsdp")),
        P("clip"),
        P("clip", ("seq", "fsdp")),
        P("clip"),
        P("clip", ("seq", "fsdp")),
        P("clip"),
        P("clip", ("seq", "fsdp")),
        P("clip"),
        P("clip", ("seq", "fsdp")),
        P("clip"),
        P("clip", "seq", "fsdp", None),
    )
    out_specs = (
        P("clip", "seq", "fsdp", None),
        P("clip", "seq", "fsdp", None),
        P("clip", None),
        P("clip", ("seq", "fsdp")),
        P("clip"),
        P("clip", ("seq", "fsdp")),
        P("clip"),
        P("clip", ("seq", "fsdp")),
        P("clip"),
        P("clip", ("seq", "fsdp")),
        P("clip"),
        P("clip", ("seq", "fsdp")),
        P("clip"),
        P("clip", ("seq", "fsdp")),
        P("clip"),
        P("clip", ("seq", "fsdp")),
        P("clip"),
        P("clip", ("seq", "fsdp")),
        P("clip"),
        P("clip", ("seq", "fsdp")),
        P("clip"),
        P("clip", ("seq", "fsdp")),
        P("clip"),
    )
    sizes = mesh.shape
    fits = (
        sizes["clip"] == 2
        and sizes["fsdp"] == 2
        and sizes["seq"] % 4 == 0
        and 16 * 3 % (2 * sizes["seq"]) == 0
        and 16 * 3 // (2 * sizes["seq"]) == 3
    )
    body = partial(ringed, sizes["seq"]) if fits else local
    return jax.shard_map(body, mesh=mesh, in_specs=in_specs, out_specs=out_specs, check_vma=False)
```

```python
from functools import partial

import jax
import jax.numpy as jnp
from jax import lax
from jax.experimental.layout import Layout, with_layout_constraint
from jax.experimental import pallas as pl
from jax.experimental.pallas import tpu as pltpu
from jax.sharding import PartitionSpec as P

HEAD = 72


norm_eps = 1e-06
space_forms = ("cfqhd,cfkhd->cfhqk", "cfhqk,cfkhd->cfqhd", "cfhqk,cfqhd->cfkhd")
time_forms = ("cqphd,ckphd->cphqk", "cphqk,ckphd->cqphd", "cphqk,cqphd->ckphd")


def norm_mod(resid, shift, scale):
    center = resid - jnp.mean(resid, axis=-1, keepdims=True)
    spread = jnp.mean(center * center, axis=-1, keepdims=True)
    normed = center * lax.rsqrt(spread + norm_eps)
    return normed * (1.0 + scale[:, None, None, :]) + shift[:, None, None, :]


def gelu_tanh(value):
    return jax.nn.gelu(value, approximate=True)


def split_heads(block):
    return block.reshape(block.shape[:-1] + (block.shape[-1] // HEAD, HEAD))


def join_heads(block):
    return block.reshape(block.shape[:-2] + (block.shape[-2] * block.shape[-1],))


def weight_grad(left, right):
    return lax.dot_general(
        left, right, (((0,), (0,)), ((), ())), preferred_element_type=jnp.float32
    )


def back_dot(grad_rows, weight):
    return lax.dot_general(
        grad_rows, weight, (((1,), (1,)), ((), ())), preferred_element_type=jnp.float32
    )


def attend(query, keys, values, forms):
    scale = HEAD ** (-0.5)
    scores = jnp.einsum(forms[0], query, keys, preferred_element_type=jnp.float32) * scale
    peak = jnp.max(scores, axis=-1, keepdims=True)
    expo = jnp.exp(scores - peak)
    total = jnp.sum(expo, axis=-1, keepdims=True)
    weights = (expo / total).astype(jnp.bfloat16)
    mixed = jnp.einsum(forms[1], weights, values, preferred_element_type=jnp.float32)
    return (mixed, peak + jnp.log(total))


def attend_back(query, keys, values, normalizer, grad_out, forms):
    scale = HEAD ** (-0.5)
    scores = jnp.einsum(forms[0], query, keys, preferred_element_type=jnp.float32) * scale
    probs = jnp.exp(scores - normalizer)
    grad_probs = jnp.einsum(forms[0], grad_out, values, preferred_element_type=jnp.float32)
    center = jnp.sum(probs * grad_probs, axis=-1, keepdims=True)
    grad_scores = (probs * (grad_probs - center)).astype(jnp.bfloat16)
    grad_query = jnp.einsum(forms[1], grad_scores, keys, preferred_element_type=jnp.float32) * scale
    grad_keys = jnp.einsum(forms[2], grad_scores, query, preferred_element_type=jnp.float32) * scale
    grad_values = jnp.einsum(
        forms[2], probs.astype(jnp.bfloat16), grad_out, preferred_element_type=jnp.float32
    )
    return (grad_query, grad_keys, grad_values)


def fetch_weights(shards):
    mod_w, mod_b, qkv_w, qv_b, proj_w, proj_b, up_w, up_b, down_w, down_b = shards
    wide = (
        lax.all_gather(mod_w, ("seq", "fsdp"), axis=1, tiled=True),
        lax.all_gather(qkv_w, ("seq", "fsdp"), axis=1, tiled=True),
        lax.all_gather(proj_w, ("seq", "fsdp"), axis=1, tiled=True),
        lax.all_gather(up_w, ("seq", "fsdp"), axis=1, tiled=True),
        lax.all_gather(down_w, ("seq", "fsdp"), axis=1, tiled=True),
    )
    whole = (
        lax.all_gather(wide[0], "clip", axis=0, tiled=True),
        lax.all_gather(wide[1], "clip", axis=0, tiled=True),
        lax.all_gather(wide[2], "clip", axis=0, tiled=True),
        lax.all_gather(wide[3], "clip", axis=0, tiled=True),
        lax.all_gather(wide[4], "clip", axis=0, tiled=True),
        lax.all_gather(mod_b, "clip", axis=0, tiled=True),
        lax.all_gather(qv_b, "clip", axis=0, tiled=True),
        lax.all_gather(proj_b, "clip", axis=0, tiled=True),
        lax.all_gather(up_b, "clip", axis=0, tiled=True),
        lax.all_gather(down_b, "clip", axis=0, tiled=True),
    )
    return (
        whole[0],
        whole[5],
        whole[1],
        whole[6],
        whole[2],
        whole[7],
        whole[3],
        whole[8],
        whole[4],
        whole[9],
    )


def layer_forward(resid, cond_act, full, spatial):
    mod_w, mod_b, qkv_w, qv_b, proj_w, proj_b, up_w, up_b, down_w, down_b = full
    width = resid.shape[-1]
    modulation = jnp.dot(cond_act, mod_w, preferred_element_type=jnp.float32) + mod_b.astype(
        jnp.float32
    )
    parts = jnp.split(modulation, 6, axis=1)
    normed_in = norm_mod(resid, parts[0], parts[1]).astype(jnp.bfloat16)
    bias_three = jnp.concatenate(
        [
            qv_b[:width].astype(jnp.float32),
            jnp.zeros((width,), jnp.float32),
            qv_b[width:].astype(jnp.float32),
        ]
    )
    projected = (
        jnp.dot(normed_in.reshape(-1, width), qkv_w, preferred_element_type=jnp.float32)
        + bias_three
    )
    projected = projected.astype(jnp.bfloat16).reshape(resid.shape[:-1] + (3 * width,))
    query = projected[..., :width]
    keys = projected[..., width : 2 * width]
    values = projected[..., 2 * width :]
    if spatial:
        keys_all, values_all = (
            lax.all_gather(keys, "fsdp", axis=2, tiled=True),
            lax.all_gather(values, "fsdp", axis=2, tiled=True),
        )
        mixed, normalizer = attend(
            split_heads(query), split_heads(keys_all), split_heads(values_all), space_forms
        )
        state = (query, keys_all, values_all, normalizer)
        att_out = join_heads(mixed.astype(jnp.bfloat16))
    else:
        keys_all, values_all = (
            lax.all_gather(keys, "seq", axis=1, tiled=True),
            lax.all_gather(values, "seq", axis=1, tiled=True),
        )
        mixed, normalizer = attend(
            split_heads(query), split_heads(keys_all), split_heads(values_all), time_forms
        )
        state = (query, keys_all, values_all, normalizer)
        att_out = join_heads(mixed.astype(jnp.bfloat16))
    proj_out = (
        jnp.dot(att_out.reshape(-1, width), proj_w, preferred_element_type=jnp.float32)
        + proj_b.astype(jnp.float32)
    ).reshape(resid.shape)
    middle = resid + parts[2][:, None, None, :] * proj_out
    normed_mid = norm_mod(middle, parts[3], parts[4]).astype(jnp.bfloat16)
    hidden = jnp.dot(
        normed_mid.reshape(-1, width), up_w, preferred_element_type=jnp.float32
    ) + up_b.astype(jnp.float32)
    active = gelu_tanh(hidden).astype(jnp.bfloat16)
    branch = (
        jnp.dot(active, down_w, preferred_element_type=jnp.float32) + down_b.astype(jnp.float32)
    ).reshape(resid.shape)
    result = middle + parts[5][:, None, None, :] * branch
    kept = (
        resid,
        parts,
        normed_in,
        state,
        att_out,
        proj_out,
        middle,
        normed_mid,
        hidden,
        active,
        branch,
    )
    return (result, kept)


def layer_backward(incoming, kept, full, spatial, grad_form):
    (
        resid,
        parts,
        normed_in,
        state,
        att_out,
        proj_out,
        middle,
        normed_mid,
        hidden,
        active,
        branch,
    ) = kept
    mod_w, mod_b, qkv_w, qv_b, proj_w, proj_b, up_w, up_b, down_w, down_b = full
    width = resid.shape[-1]
    grad_gate2 = jnp.sum(incoming * branch, axis=(1, 2))
    grad_branch = (parts[5][:, None, None, :] * incoming).astype(jnp.bfloat16).reshape(-1, width)
    grad_down = grad_form(active, grad_branch)
    bias_down = jnp.sum(grad_branch, axis=0, dtype=jnp.float32)
    grad_active = back_dot(grad_branch, down_w)
    unused, gelu_back = jax.vjp(gelu_tanh, hidden)
    grad_hidden = gelu_back(grad_active)[0].astype(jnp.bfloat16)
    grad_up = grad_form(normed_mid.reshape(-1, width), grad_hidden)
    bias_up = jnp.sum(grad_hidden, axis=0, dtype=jnp.float32)
    grad_second = back_dot(grad_hidden, up_w).reshape(resid.shape)
    unused, norm_back_mid = jax.vjp(norm_mod, middle, parts[3], parts[4])
    grad_from, grad_shift2, grad_scale2 = norm_back_mid(grad_second)
    grad_middle = incoming + grad_from
    grad_gate1 = jnp.sum(grad_middle * proj_out, axis=(1, 2))
    grad_proj = (parts[2][:, None, None, :] * grad_middle).astype(jnp.bfloat16).reshape(-1, width)
    grad_projw = grad_form(att_out.reshape(-1, width), grad_proj)
    bias_proj = jnp.sum(grad_proj, axis=0, dtype=jnp.float32)
    grad_att = back_dot(grad_proj, proj_w).astype(jnp.bfloat16).reshape(resid.shape)
    query_s, keys_s, values_s, normalizer = state
    if spatial:
        query_terms, key_terms, value_terms = attend_back(
            split_heads(query_s),
            split_heads(keys_s),
            split_heads(values_s),
            normalizer,
            split_heads(grad_att),
            space_forms,
        )
        grad_keys, grad_values = (
            lax.psum_scatter(
                join_heads(key_terms).astype(jnp.bfloat16), "fsdp", scatter_dimension=2, tiled=True
            ).astype(jnp.float32),
            lax.psum_scatter(
                join_heads(value_terms).astype(jnp.bfloat16),
                "fsdp",
                scatter_dimension=2,
                tiled=True,
            ).astype(jnp.float32),
        )
        grad_query = join_heads(query_terms)
    else:
        query_terms, key_terms, value_terms = attend_back(
            split_heads(query_s),
            split_heads(keys_s),
            split_heads(values_s),
            normalizer,
            split_heads(grad_att),
            time_forms,
        )
        grad_keys, grad_values = (
            lax.psum_scatter(
                join_heads(key_terms).astype(jnp.bfloat16), "seq", scatter_dimension=1, tiled=True
            ).astype(jnp.float32),
            lax.psum_scatter(
                join_heads(value_terms).astype(jnp.bfloat16), "seq", scatter_dimension=1, tiled=True
            ).astype(jnp.float32),
        )
        grad_query = join_heads(query_terms)
    grad_three = jnp.concatenate(
        [
            grad_query.astype(jnp.bfloat16),
            grad_keys.astype(jnp.bfloat16),
            grad_values.astype(jnp.bfloat16),
        ],
        axis=3,
    ).reshape(-1, 3 * width)
    grad_qkvw = grad_form(normed_in.reshape(-1, width), grad_three)
    bias_qv = jnp.concatenate(
        [
            jnp.sum(grad_three[:, :width], axis=0, dtype=jnp.float32),
            jnp.sum(grad_three[:, 2 * width :], axis=0, dtype=jnp.float32),
        ]
    )
    grad_first = back_dot(grad_three, qkv_w).reshape(resid.shape)
    unused, norm_back_in = jax.vjp(norm_mod, resid, parts[0], parts[1])
    grad_from_in, grad_shift1, grad_scale1 = norm_back_in(grad_first)
    grad_resid = grad_middle + grad_from_in
    grad_modulation = jnp.concatenate(
        [grad_shift1, grad_scale1, grad_gate1, grad_shift2, grad_scale2, grad_gate2], axis=1
    )
    return (
        grad_resid,
        grad_modulation,
        (grad_qkvw, grad_projw, grad_up, grad_down),
        (bias_qv, bias_proj, bias_up, bias_down),
    )


def local(
    tokens,
    condition,
    space_adaw,
    space_adab,
    space_qkv,
    space_qvb,
    space_proj,
    space_projb,
    space_up,
    space_upb,
    space_down,
    space_downb,
    time_adaw,
    time_adab,
    time_qkv,
    time_qvb,
    time_proj,
    time_projb,
    time_up,
    time_upb,
    time_down,
    time_downb,
    cotangent,
):
    cond_in = condition.astype(jnp.float32)
    cond_act = jax.nn.silu(cond_in).astype(jnp.bfloat16)
    layers = (
        (
            space_adaw,
            space_adab,
            space_qkv,
            space_qvb,
            space_proj,
            space_projb,
            space_up,
            space_upb,
            space_down,
            space_downb,
        ),
        (
            time_adaw,
            time_adab,
            time_qkv,
            time_qvb,
            time_proj,
            time_projb,
            time_up,
            time_upb,
            time_down,
            time_downb,
        ),
    )
    resid = tokens.astype(jnp.float32)
    gathered = []
    saved = []
    for index in range(2):
        full = fetch_weights(layers[index])
        resid, kept = layer_forward(resid, cond_act, full, index == 0)
        gathered.append(full)
        saved.append(kept)
    output = resid.astype(jnp.bfloat16)
    incoming = cotangent.astype(jnp.float32)
    grad_act = jnp.zeros(cond_in.shape, jnp.float32)
    results = [None, None]
    for index in (1, 0):
        full = gathered[index]
        incoming, grad_mod, weight_terms, bias_terms = layer_backward(
            incoming, saved[index], full, index == 0, weight_grad
        )
        summed = (
            lax.psum(grad_mod.astype(jnp.bfloat16), ("seq", "fsdp")).astype(jnp.float32),
            lax.psum(bias_terms[0].astype(jnp.bfloat16), ("seq", "fsdp")).astype(jnp.float32),
            lax.psum(bias_terms[1].astype(jnp.bfloat16), ("seq", "fsdp")).astype(jnp.float32),
            lax.psum(bias_terms[2].astype(jnp.bfloat16), ("seq", "fsdp")).astype(jnp.float32),
            lax.psum(bias_terms[3].astype(jnp.bfloat16), ("seq", "fsdp")).astype(jnp.float32),
        )
        mod_low = summed[0].astype(jnp.bfloat16)
        grad_act = grad_act + back_dot(mod_low, full[0])
        columns = layers[index][0].shape[1]
        mod_cols = lax.dynamic_slice_in_dim(
            mod_low, lax.axis_index(("seq", "fsdp")) * columns, columns, 1
        )
        ada_cols = weight_grad(cond_act, mod_cols)
        ada_bias = jnp.sum(mod_low, axis=0, dtype=jnp.float32)
        row_parts = (
            lax.psum_scatter(
                ada_cols.astype(jnp.bfloat16), "clip", scatter_dimension=0, tiled=True
            ).astype(jnp.float32),
            lax.psum_scatter(
                weight_terms[0].astype(jnp.bfloat16), "clip", scatter_dimension=0, tiled=True
            ).astype(jnp.float32),
            lax.psum_scatter(
                weight_terms[1].astype(jnp.bfloat16), "clip", scatter_dimension=0, tiled=True
            ).astype(jnp.float32),
            lax.psum_scatter(
                weight_terms[2].astype(jnp.bfloat16), "clip", scatter_dimension=0, tiled=True
            ).astype(jnp.float32),
            lax.psum_scatter(
                weight_terms[3].astype(jnp.bfloat16), "clip", scatter_dimension=0, tiled=True
            ).astype(jnp.float32),
            lax.psum_scatter(
                ada_bias.astype(jnp.bfloat16), "clip", scatter_dimension=0, tiled=True
            ).astype(jnp.float32),
            lax.psum_scatter(
                summed[1].astype(jnp.bfloat16), "clip", scatter_dimension=0, tiled=True
            ).astype(jnp.float32),
            lax.psum_scatter(
                summed[2].astype(jnp.bfloat16), "clip", scatter_dimension=0, tiled=True
            ).astype(jnp.float32),
            lax.psum_scatter(
                summed[3].astype(jnp.bfloat16), "clip", scatter_dimension=0, tiled=True
            ).astype(jnp.float32),
            lax.psum_scatter(
                summed[4].astype(jnp.bfloat16), "clip", scatter_dimension=0, tiled=True
            ).astype(jnp.float32),
        )
        col_parts = (
            lax.psum_scatter(
                row_parts[1].astype(jnp.bfloat16), ("seq", "fsdp"), scatter_dimension=1, tiled=True
            ).astype(jnp.float32),
            lax.psum_scatter(
                row_parts[2].astype(jnp.bfloat16), ("seq", "fsdp"), scatter_dimension=1, tiled=True
            ).astype(jnp.float32),
            lax.psum_scatter(
                row_parts[3].astype(jnp.bfloat16), ("seq", "fsdp"), scatter_dimension=1, tiled=True
            ).astype(jnp.float32),
            lax.psum_scatter(
                row_parts[4].astype(jnp.bfloat16), ("seq", "fsdp"), scatter_dimension=1, tiled=True
            ).astype(jnp.float32),
        )
        results[index] = (
            row_parts[0],
            row_parts[5],
            col_parts[0],
            row_parts[6],
            col_parts[1],
            row_parts[7],
            col_parts[2],
            row_parts[8],
            col_parts[3],
            row_parts[9],
        )
    unused, silu_back = jax.vjp(jax.nn.silu, cond_in)
    condition_grad = silu_back(grad_act)[0]
    return (output, incoming, condition_grad) + results[0] + results[1]


SWAP = [(0, 1), (1, 0)]
BF = jnp.bfloat16
F32 = jnp.float32


def swap_core(value):
    return lax.ppermute(value, "fsdp", SWAP)


def swap_clip(value):
    return lax.ppermute(value, "clip", SWAP)


class Ring:
    def __init__(self, size):
        half = size // 2
        self.size = size
        order = [2 * row for row in range(half)] + [2 * row + 1 for row in reversed(range(half))]
        self.ahead = [(order[at], order[(at + 1) % size]) for at in range(size)]
        self.behind = [(to, frm) for frm, to in self.ahead]
        here = lax.axis_index("seq")
        row, column = here // 2, here % 2
        self.position = jnp.where(column == 0, row, size - 1 - row)

    def chip(self, offset):
        at = (self.position + offset + self.size) % self.size
        return jnp.where(at < self.size // 2, 2 * at, 2 * (self.size - 1 - at) + 1)

    def send_ahead(self, value):
        return lax.ppermute(value, "seq", self.ahead)

    def send_behind(self, value):
        return lax.ppermute(value, "seq", self.behind)


def after(value, *marks):
    if not marks:
        return value
    return lax.optimization_barrier((value, *marks))[0]


def flip_seat(value, bit, size):
    return lax.ppermute(value, "seq", [(at, at ^ bit) for at in range(size)])


def sum_seats(value, size, mark=()):
    bit = 1
    while bit < size:
        value = value + flip_seat(after(value, *mark[:1]), bit, size)
        mark = mark[1:]
        bit *= 2
    return value


def sum_all(value, size, marks=()):
    value = after(value, *marks[:1])
    value = value + swap_core(value)
    value = sum_seats(value, size, marks[1:])
    return value + swap_clip(value)


def join_message(upper, lower):
    width = upper.shape[1]
    if lower.shape[1] != width:
        half = lower.shape[0] // 2
        lower = jnp.concatenate([lower[:half], lower[half:]], axis=1)
    return jnp.concatenate([upper, lower], axis=0)


def store_message(message, upper_ref, lower_ref, where, upper_rows):
    upper_ref[where] = message[:upper_rows].astype(upper_ref.dtype)
    lower = message[upper_rows:].astype(lower_ref.dtype)
    if lower_ref.shape[2] == message.shape[1]:
        lower_ref[where] = lower
    else:
        half = lower_ref.shape[1] // 2
        lower_ref[where, :half] = lower[:, : lower_ref.shape[2]]
        lower_ref[where, half:] = lower[:, lower_ref.shape[2] :]


def whole_spec(shape):
    return pl.BlockSpec(shape, lambda at, seats: (0,) * len(shape))


def seat_spec(shape, which):
    return pl.BlockSpec(
        (1,) + tuple(shape[1:]), lambda at, seats: (seats[which],) + (0,) * (len(shape) - 1)
    )


def message_call(body, seats, inputs, in_specs, outs, moved):
    return pl.pallas_call(
        body,
        grid_spec=pltpu.PrefetchScalarGridSpec(
            num_scalar_prefetch=1,
            grid=(1,),
            in_specs=in_specs,
            out_specs=[whole_spec(item.shape) for item in outs],
        ),
        out_shape=outs,
        cost_estimate=pl.CostEstimate(flops=moved, bytes_accessed=moved * 4, transcendentals=0),
    )(seats, *inputs)


def assemble_body(seats, *refs, count):
    messages, (upper_ref, lower_ref) = refs[: count + 1], refs[count + 1 :]
    rows = upper_ref.shape[1]
    for at in range(count - 1):
        store_message(messages[at][...], upper_ref, lower_ref, seats[at], rows)
    last = jnp.concatenate([messages[count - 1][...], messages[count][...]], axis=0)
    store_message(last, upper_ref, lower_ref, seats[count - 1], rows)


def ring_gather(ring, message, upper_rows, lower_shape, *marks):
    message = after(message, *marks)
    steps = ring.size // 2
    half = message.shape[0] // 2
    front, back = message, message
    fronts, backs = [], []
    for step in range(1, steps):
        front, back = ring.send_ahead(front), ring.send_behind(back)
        fronts.append(front)
        backs.append(back)
    low_part, high_part = ring.send_ahead(front[:half]), ring.send_behind(back[half:])
    messages = [message] + fronts + backs + [low_part, high_part]
    offsets = [0] + [-step for step in range(1, steps)] + list(range(1, steps + 1))
    seats = jnp.stack([ring.chip(offset) for offset in offsets])
    outs = [
        jax.ShapeDtypeStruct((ring.size, upper_rows, message.shape[1]), message.dtype),
        jax.ShapeDtypeStruct((ring.size,) + lower_shape, message.dtype),
    ]
    upper, lower = message_call(
        partial(assemble_body, count=ring.size),
        seats,
        messages,
        [whole_spec(item.shape) for item in messages],
        outs,
        ring.size * message.size,
    )
    return (upper.reshape(-1, upper.shape[2]), lower.reshape(-1, lower.shape[2])), fronts


def add_message(out, upper, lower, got, span):
    rows = upper.shape[1]
    width = upper.shape[2]
    start, stop = span
    if start < rows:
        end = min(rows, stop)
        mine = upper[0, start:end]
        out[start:end] = mine if got is None else mine + got[start - got.start : end - got.start]
    if stop > rows:
        begin = max(start, rows)
        if lower.shape[2] == width:
            mine = lower[0, begin - rows : stop - rows]
        else:
            half = lower.shape[1] // 2
            mine = jnp.concatenate(
                [lower[0, begin - rows : stop - rows], lower[0, half + begin - rows : half + stop - rows]],
                axis=1,
            )
        out[begin:stop] = mine if got is None else mine + got[begin - got.start : stop - got.start]


class Span:
    def __init__(self, ref, start):
        self.ref = ref
        self.start = start
        self.stop = start + ref.shape[0]

    def __getitem__(self, rows):
        return self.ref[rows]

    def __setitem__(self, rows, value):
        self.ref[rows.start - self.start : rows.stop - self.start] = value


def open_body(seats, upper, lower, low_ref, high_ref):
    half = low_ref.shape[0]
    add_message(Span(low_ref, 0), upper, lower, None, (0, half))
    add_message(Span(high_ref, half), upper, lower, None, (half, half + high_ref.shape[0]))


def add_body(seats, front_in, back_in, upper_f, lower_f, upper_b, lower_b, front, back):
    total, got = front.shape[0], front_in.shape[0]
    add_message(front, upper_f, lower_f, Span(front_in, 0), (0, got))
    if got < total:
        add_message(front, upper_f, lower_f, None, (got, total))
        add_message(back, upper_b, lower_b, None, (0, total - got))
    add_message(back, upper_b, lower_b, Span(back_in, total - got), (total - got, total))


def clip_halves(message, folded_from):
    half = message.shape[1] // 2
    if folded_from is None:
        return (message[:, :half], message[:, half:])
    quarter = half // 2
    top, low = message[:folded_from], message[folded_from:]
    return tuple(
        jnp.concatenate(
            [
                top[:, at * half : (at + 1) * half],
                jnp.concatenate(
                    [
                        low[:, at * quarter : (at + 1) * quarter],
                        low[:, half + at * quarter : half + (at + 1) * quarter],
                    ],
                    axis=1,
                ),
            ],
            axis=0,
        )
        for at in range(2)
    )


def close_body(seats, front_in, back_in, upper_in, lower_in, keep_ref, give_ref, *, folded_from):
    mine = join_message(upper_in[0].astype(F32), lower_in[0].astype(F32))
    total = mine + front_in[...].astype(F32) + back_in[...].astype(F32)
    zero, one = clip_halves(total, folded_from)
    first = seats[1] == 0
    keep_ref[...] = jnp.where(first, zero, one)
    give_ref[...] = jnp.where(first, one, zero).astype(give_ref.dtype)


def ring_scatter(ring, upper, lower):
    steps = ring.size // 2
    upper = upper.reshape(ring.size, -1, upper.shape[1])
    lower = lower.reshape(ring.size, -1, lower.shape[1])
    width = upper.shape[2]
    rows = upper.shape[1] + lower.shape[1] * lower.shape[2] // width
    half = rows // 2
    moved = rows * width
    sent = jax.ShapeDtypeStruct((rows, width), BF)
    part = jax.ShapeDtypeStruct((half, width), BF)
    pair = lambda which: [seat_spec(upper.shape, which), seat_spec(lower.shape, which)]
    front, back = message_call(
        open_body,
        jnp.stack([ring.chip(steps)]),
        (upper, lower),
        pair(0),
        [part, part],
        moved,
    )
    marks = []
    for step in range(steps - 1, 0, -1):
        front, back = ring.send_ahead(front), ring.send_behind(back)
        front, back = message_call(
            add_body,
            jnp.stack([ring.chip(step), ring.chip(-step)]),
            (front, back, upper, lower, upper, lower),
            [whole_spec(front.shape), whole_spec(back.shape)] + pair(0) + pair(1),
            [sent, sent],
            2 * moved,
        )
        marks.append(front)
    front, back = ring.send_ahead(front), ring.send_behind(back)
    keep, give = message_call(
        partial(close_body, folded_from=upper.shape[1] if lower.shape[2] != width else None),
        jnp.stack([ring.chip(0), lax.axis_index("clip")]),
        (front, back, upper, lower),
        [whole_spec(front.shape), whole_spec(back.shape)] + pair(0),
        [
            jax.ShapeDtypeStruct((rows, width // 2), F32),
            jax.ShapeDtypeStruct((rows, width // 2), BF),
        ],
        2 * moved,
    )
    return (keep, give), marks


def pick(flag, when_zero, when_one):
    return jnp.where(flag == 0, when_zero, when_one)


def order_two(flag, mine, other, axis):
    return pick(
        flag,
        jnp.concatenate([mine, other], axis=axis),
        jnp.concatenate([other, mine], axis=axis),
    )


def stack_two(flag, mine, other, axis):
    return pick(flag, jnp.stack([mine, other], axis), jnp.stack([other, mine], axis))


def flat_call(body, flags, inputs, outs):
    moved = sum(item.size for item in inputs)
    return pl.pallas_call(
        body,
        grid_spec=pltpu.PrefetchScalarGridSpec(
            num_scalar_prefetch=1,
            grid=(1,),
            in_specs=[whole_spec(item.shape) for item in inputs],
            out_specs=[whole_spec(shape) for shape, kind in outs],
        ),
        out_shape=[jax.ShapeDtypeStruct(shape, kind) for shape, kind in outs],
        cost_estimate=pl.CostEstimate(flops=moved, bytes_accessed=moved * 4, transcendentals=0),
    )(flags, *inputs)


def choose(flag, zero, one):
    return jnp.where(flag == 0, zero, one)


def columns_of(value, starts, size):
    return jnp.concatenate([value[:, start : start + size] for start in starts], axis=1)


class AttentionPiece:
    def __init__(self, qkv_w, proj_w):
        self.depth, self.columns = qkv_w.shape
        self.proj_columns = proj_w.shape[1]
        self.heads = proj_w.shape[0] // HEAD
        self.share = proj_w.shape[0] // 2
        self.weights = [qkv_w.T, proj_w.T]
        self.rows = self.columns + self.proj_columns
        ends = ((2 * HEAD, self.depth), BF)
        mid = ((HEAD, self.depth), BF)
        piece = ((self.proj_columns, self.share), BF)
        self.first_outs = [ends, piece, mid, piece]
        self.first_gives = (2, 3)
        self.half_outs = [((self.rows, self.depth), BF)]
        self.half_give = 0
        self.last_outs = [((self.rows, 2 * self.depth), BF)]
        self.split_outs = [
            ((2 * HEAD, self.depth), F32),
            ((self.proj_columns, self.share), F32),
            ((HEAD, self.depth), F32),
            ((self.proj_columns, self.share), F32),
        ]
        self.split_gives = (2, 3)
        self.done_outs = [(item.shape, F32) for item in self.weights]

    def first(self, clip, core, qkv_w, proj_w):
        turned = qkv_w[...].astype(F32)
        proj = proj_w[...].astype(F32)
        even = columns_of(proj, range(0, self.heads * HEAD, 2 * HEAD), HEAD)
        odd = columns_of(proj, range(HEAD, self.heads * HEAD, 2 * HEAD), HEAD)
        ends = jnp.concatenate([turned[:HEAD], turned[2 * HEAD :]], axis=0)
        return (ends, choose(core, even, odd), turned[HEAD : 2 * HEAD], choose(core, odd, even))

    def half(self, clip, core, ends, keep, mid, got):
        ends, keep, mid, got = (item[...].astype(F32) for item in (ends, keep, mid, got))
        qkv = choose(
            core, jnp.concatenate([ends, mid], axis=0), jnp.concatenate([mid, ends], axis=0)
        )
        proj = choose(
            core, jnp.concatenate([keep, got], axis=1), jnp.concatenate([got, keep], axis=1)
        )
        return (jnp.concatenate([qkv, proj], axis=0),)

    def last(self, clip, core, mine, got):
        mine, got = mine[...].astype(F32), got[...].astype(F32)
        zero, one = choose(clip, mine, got), choose(clip, got, mine)
        cut, share = self.columns, self.share
        top = jnp.concatenate([zero[:cut], one[:cut]], axis=1)
        low = jnp.concatenate(
            [zero[cut:, :share], one[cut:, :share], zero[cut:, share:], one[cut:, share:]], axis=1
        )
        return (jnp.concatenate([top, low], axis=0),)

    def split(self, clip, core, keep, got):
        total = keep[...] + got[...].astype(F32)
        first, second, third = (total[at : at + HEAD] for at in range(0, self.columns, HEAD))
        low = total[self.columns :]
        zero, one = low[:, : self.share], low[:, self.share :]
        stay = jnp.concatenate([choose(core, first, second), choose(core, second, third)], axis=0)
        return (stay, choose(core, zero, one), choose(core, third, first), choose(core, one, zero))

    def done(self, clip, core, stay, keep, mid, got):
        stay = stay[...]
        qkv = jnp.concatenate([stay[:HEAD], mid[...], stay[HEAD:]], axis=0)
        keep, got = keep[...], got[...]
        even, odd = choose(core, keep, got), choose(core, got, keep)
        proj = jnp.concatenate(
            [
                part[:, at : at + HEAD]
                for at in range(0, self.share, HEAD)
                for part in (even, odd)
            ],
            axis=1,
        )
        return (qkv, proj)


class FeedPiece:
    def __init__(self, up_w, down_w):
        self.depth, self.columns = up_w.shape
        self.cell = self.columns // 2
        self.down_rows, self.down_columns = down_w.shape
        self.groups = self.down_rows // (4 * self.cell)
        self.weights = [up_w.T, down_w.T]
        self.rows = self.cell + 2 * self.down_columns
        up = ((self.cell, self.depth), BF)
        down = ((2 * self.down_columns, self.depth), BF)
        self.first_outs = [up, up, down, down]
        self.first_gives = (3,)
        self.half_outs = [((self.rows, self.depth), BF)] * 2
        self.half_give = 1
        self.last_outs = [((self.rows, 2 * self.depth), BF)]
        self.split_outs = [
            (self.weights[0].shape, F32),
            ((2 * self.down_columns, self.depth), F32),
            ((2 * self.down_columns, self.depth), F32),
        ]
        self.split_gives = (2,)
        self.done_outs = [(self.weights[1].shape, F32)]

    def first(self, clip, core, up_w, down_w):
        turned = up_w[...].astype(F32)
        zero, one = turned[: self.cell], turned[self.cell :]
        down = down_w[...].astype(F32)
        step = 4 * self.cell

        def part(of_core, of_clip):
            begin = (2 * of_core + of_clip) * self.cell
            return columns_of(down, range(begin, self.down_rows, step), self.cell)

        parts = [jnp.concatenate([part(at, 0), part(at, 1)], axis=0) for at in range(2)]
        return (
            choose(clip, zero, one),
            choose(clip, one, zero),
            choose(core, parts[0], parts[1]),
            choose(core, parts[1], parts[0]),
        )

    def half(self, clip, core, up_keep, up_give, keep, got):
        up_keep, up_give, keep, got = (
            item[...].astype(F32) for item in (up_keep, up_give, keep, got)
        )
        zero, one = choose(core, keep, got), choose(core, got, keep)
        cut = self.down_columns
        downs = [
            jnp.concatenate([zero[at * cut : (at + 1) * cut], one[at * cut : (at + 1) * cut]], axis=0)
            for at in range(2)
        ]
        stay = jnp.concatenate([up_keep, choose(clip, downs[0], downs[1])], axis=0)
        give = jnp.concatenate([up_give, choose(clip, downs[1], downs[0])], axis=0)
        return (stay, give)

    def last(self, clip, core, mine, unused, got):
        mine, got = mine[...].astype(F32), got[...].astype(F32)
        return (
            jnp.concatenate([choose(clip, mine, got), choose(clip, got, mine)], axis=1),
        )

    def split(self, clip, core, keep, got):
        keep, got = keep[...], got[...].astype(F32)
        zero, one = choose(clip, keep, got), choose(clip, got, keep)
        cell, cut = self.cell, self.down_columns
        up = jnp.concatenate([zero[:cell], one[:cell]], axis=0)
        downs = [
            jnp.concatenate(
                [item[cell + at * cut : cell + (at + 1) * cut] for item in (zero, one)], axis=0
            )
            for at in range(2)
        ]
        return (up, choose(core, downs[0], downs[1]), choose(core, downs[1], downs[0]))

    def done(self, clip, core, keep, got):
        keep, got = keep[...], got[...]
        zero, one = choose(core, keep, got), choose(core, got, keep)
        cut, cell = self.down_columns, self.cell
        cells = {}
        for of_core, value in enumerate((zero, one)):
            for of_clip in range(2):
                cells[of_core, of_clip] = value[of_clip * cut : (of_clip + 1) * cut]
        down = jnp.concatenate(
            [
                cells[of_core, of_clip][:, at * cell : (at + 1) * cell]
                for at in range(self.groups)
                for of_core in range(2)
                for of_clip in range(2)
            ],
            axis=1,
        )
        return (down,)


def stage(name, pieces, flags, inputs):
    outs = [getattr(piece, name + "_outs") for piece in pieces]
    counts = [len(item) for item in inputs]

    def body(flags_ref, *refs):
        clip, core = flags_ref[0], flags_ref[1]
        at, out_at = 0, sum(counts)
        for piece, count, out in zip(pieces, counts, outs):
            values = getattr(piece, name)(clip, core, *refs[at : at + count])
            for ref, value in zip(refs[out_at : out_at + len(out)], values):
                ref[...] = value.astype(ref.dtype)
            at += count
            out_at += len(out)

    flat = flat_call(
        body, flags, [x for item in inputs for x in item], [x for item in outs for x in item]
    )
    results = []
    for out in outs:
        results.append(list(flat[: len(out)]))
        flat = flat[len(out) :]
    return results


def swap_some(pieces, kind, results):
    for piece, result in zip(pieces, results):
        for at in getattr(piece, kind + "_gives"):
            result[at] = swap_core(result[at])
    return results


def make_messages(pieces, flags, weights):
    results = swap_some(pieces, "first", stage("first", pieces, flags, weights))
    halves = stage("half", pieces, flags, results)
    gives = [half[piece.half_give] for piece, half in zip(pieces, halves)]
    got = swap_clip(jnp.concatenate(gives, axis=0) if len(gives) > 1 else gives[0])
    start = 0
    for half, give in zip(halves, gives):
        half.append(got[start : start + give.shape[0]])
        start += give.shape[0]
    return [item[0] for item in stage("last", pieces, flags, halves)]


def make_gradients(pieces, flags, sums):
    gives = [give for keep, give in sums]
    got = swap_clip(jnp.concatenate(gives, axis=0) if len(gives) > 1 else gives[0])
    inputs, start = [], 0
    for keep, give in sums:
        inputs.append([keep, got[start : start + give.shape[0]]])
        start += give.shape[0]
    parts = swap_some(pieces, "split", stage("split", pieces, flags, inputs))
    heads = [part[:1] if isinstance(piece, FeedPiece) else [] for piece, part in zip(pieces, parts)]
    rests = [part[1:] if isinstance(piece, FeedPiece) else part for piece, part in zip(pieces, parts)]
    dones = stage("done", pieces, flags, rests)
    return [[item.T for item in head + done] for head, done in zip(heads, dones)]


def softmax_rows(query, keys, masked, group):
    scores = lax.dot_general(
        query, keys, (((1,), (1,)), ((), ())), preferred_element_type=F32
    ) * HEAD ** (-0.5)
    if masked:
        rows = lax.broadcasted_iota(jnp.int32, scores.shape, 0)
        cols = lax.broadcasted_iota(jnp.int32, scores.shape, 1)
        scores = jnp.where(rows % group == cols % group, scores, -1e30)
    peak = jnp.max(scores, axis=-1, keepdims=True)
    expo = jnp.exp(scores - peak)
    return expo / jnp.sum(expo, axis=-1, keepdims=True)


def load_rows(ref):
    value = ref[...]
    return value.reshape(-1, value.shape[-1])


def attention_kernel(qkv_ref, out_ref, *, masked, group):
    block = load_rows(qkv_ref)
    width = block.shape[1] // 3
    outs = []
    for at in range(0, width, HEAD):
        probs = softmax_rows(
            block[:, at : at + HEAD], block[:, width + at : width + at + HEAD], masked, group
        ).astype(BF)
        outs.append(
            jnp.dot(
                probs,
                block[:, 2 * width + at : 2 * width + at + HEAD],
                preferred_element_type=F32,
            ).astype(BF)
        )
    out_ref[...] = jnp.concatenate(outs, axis=1).reshape(out_ref.shape)


def attention_back_kernel(qkv_ref, grad_ref, out_ref, *, masked, group):
    block = load_rows(qkv_ref)
    grads = load_rows(grad_ref)
    width = block.shape[1] // 3
    scale = HEAD ** (-0.5)
    grad_q, grad_k, grad_v = [], [], []
    for at in range(0, width, HEAD):
        query = block[:, at : at + HEAD]
        keys = block[:, width + at : width + at + HEAD]
        values = block[:, 2 * width + at : 2 * width + at + HEAD]
        grad = grads[:, at : at + HEAD]
        probs = softmax_rows(query, keys, masked, group)
        grad_probs = lax.dot_general(
            grad, values, (((1,), (1,)), ((), ())), preferred_element_type=F32
        )
        center = jnp.sum(probs * grad_probs, axis=-1, keepdims=True)
        grad_scores = (probs * (grad_probs - center)).astype(BF)
        grad_q.append(
            (jnp.dot(grad_scores, keys, preferred_element_type=F32) * scale).astype(BF)
        )
        grad_k.append((weight_grad(grad_scores, query) * scale).astype(BF))
        grad_v.append(weight_grad(probs.astype(BF), grad).astype(BF))
    out_ref[...] = jnp.concatenate(grad_q + grad_k + grad_v, axis=1).reshape(out_ref.shape)


def group_spec(spatial, frames, places, width):
    if spatial:
        return pl.BlockSpec((2, 1, places, width), lambda at: (0, at, 0, 0))
    return pl.BlockSpec((1, 1, frames * places, width), lambda at: (at, 0, 0, 0))


def group_shape(spatial, frames, places, width):
    if spatial:
        return (2, frames, places, width)
    return (2, 1, frames * places, width)


def attention_call(body, inputs, out_width, spatial, frames, places, group, flops):
    steps = frames if spatial else 2
    specs = [group_spec(spatial, frames, places, item.shape[-1]) for item in inputs]
    shaped = [
        item.reshape(group_shape(spatial, frames, places, item.shape[-1])) for item in inputs
    ]
    tokens = inputs[0].shape[0]
    out = pl.pallas_call(
        partial(body, masked=not spatial, group=group),
        grid=(steps,),
        in_specs=specs,
        out_specs=group_spec(spatial, frames, places, out_width),
        out_shape=jax.ShapeDtypeStruct(group_shape(spatial, frames, places, out_width), BF),
        cost_estimate=pl.CostEstimate(
            flops=flops, bytes_accessed=tokens * 2 * 4 * out_width, transcendentals=tokens * 2048
        ),
    )(*shaped)
    return out.reshape(tokens, out_width)


def rows_call(body, rows, inputs, params, outs, sums):
    block = rows // 2
    width = params[0].shape[-1]

    def kernel(*refs):
        at = len(inputs) + len(params)
        values = [ref[...].astype(F32) for ref in refs[:at]]
        results, totals = body(*values)
        for ref, value in zip(refs[at:], results):
            ref[...] = value.astype(ref.dtype)
        if sums:
            sum_ref = refs[-1]

            @pl.when(pl.program_id(0) == 0)
            def _():
                sum_ref[...] = jnp.zeros_like(sum_ref)

            for where, value in enumerate(totals):
                sum_ref[where : where + 1] += jnp.sum(value, axis=0, keepdims=True)

    row_spec = pl.BlockSpec((block, width), lambda at: (at, 0))
    param_specs = [pl.BlockSpec(item.shape, lambda at: (0, 0)) for item in params]
    shapes = [jax.ShapeDtypeStruct((rows, width), kind) for kind in outs]
    specs = [row_spec] * len(outs)
    if sums:
        shapes.append(jax.ShapeDtypeStruct((8, width), F32))
        specs.append(pl.BlockSpec((8, width), lambda at: (0, 0)))
    moved = rows * width * 4 * (len(inputs) + len(outs))
    return pl.pallas_call(
        kernel,
        grid=(rows // block,),
        in_specs=[row_spec] * len(inputs) + param_specs,
        out_specs=specs,
        out_shape=shapes,
        cost_estimate=pl.CostEstimate(flops=10 * moved, bytes_accessed=moved, transcendentals=rows),
    )(*inputs, *params)


def normalize(value):
    center = value - jnp.mean(value, axis=-1, keepdims=True)
    spread = jnp.mean(center * center, axis=-1, keepdims=True)
    rate = lax.rsqrt(spread + norm_eps)
    return (center * rate, rate)


def norm_back(grad, normed, rate, scale):
    inner = grad * (1.0 + scale)
    return rate * (
        inner
        - jnp.mean(inner, axis=-1, keepdims=True)
        - normed * jnp.mean(inner * normed, axis=-1, keepdims=True)
    )


def first_rows(resid, mods):
    return (normalize(resid)[0] * (1.0 + mods[1:2]) + mods[0:1],), ()


def middle_rows(near, from_core, resid, mods, biases):
    attended = near + from_core + biases[0:1]
    middle = resid + mods[2:3] * attended
    second = normalize(middle)[0] * (1.0 + mods[4:5]) + mods[3:4]
    return (attended, middle, second), ()


def result_rows(near, from_core, from_clip, middle, mods, biases):
    branch = near + from_core + from_clip + biases[1:2]
    return (branch, middle + mods[5:6] * branch), ()


def open_rows(incoming, branch, mods):
    grad = (mods[5:6] * incoming).astype(BF)
    return (grad,), (incoming * branch, grad.astype(F32))


def middle_back_rows(near, from_core, from_clip, incoming, middle, attended, mods):
    grad = near + from_core + from_clip
    normed, rate = normalize(middle)
    grad_middle = incoming + norm_back(grad, normed, rate, mods[4:5])
    grad_att = (mods[2:3] * grad_middle).astype(BF)
    return (grad_middle, grad_att), (
        grad,
        grad * normed,
        grad_middle * attended,
        grad_att.astype(F32),
    )


def first_back_rows(near, from_core, grad_middle, resid, mods):
    grad = near + from_core
    normed, rate = normalize(resid)
    return (grad_middle + norm_back(grad, normed, rate, mods[1:2]),), (grad, grad * normed)


def row_major(value):
    return with_layout_constraint(value, Layout(tuple(range(value.ndim))))


def nt_dot(rows, weight):
    return lax.dot_general(
        rows, weight, (((1,), (1,)), ((), ())), preferred_element_type=F32
    )


def nn_dot(rows, weight):
    return jnp.dot(rows, weight, preferred_element_type=F32)


def from_core_half(partial_sum):
    return swap_core(partial_sum[partial_sum.shape[0] // 2 :].astype(BF))


def from_clip_rows(far):
    half = far.shape[0] // 2
    return swap_clip((far[:half] + from_core_half(far).astype(F32)).astype(BF))


def gather_four(mine):
    across = swap_clip(mine)
    near = jnp.concatenate([mine, swap_core(mine)], axis=0)
    far = jnp.concatenate([across, swap_core(across)], axis=0)
    return (near, far)


def gelu_both(hidden):
    rate = 0.7978845608028654
    bend = 0.044715
    square = hidden * hidden
    tanh = jnp.tanh(rate * hidden * (1.0 + bend * square))
    value = 0.5 * hidden * (1.0 + tanh)
    slope = 0.5 * (1.0 + tanh) + 0.5 * hidden * (1.0 - tanh * tanh) * rate * (
        1.0 + 3.0 * bend * square
    )
    return (value.astype(BF), slope.astype(BF))


def block_forward(resid, parts, attn_w, mlp_w, biases, spatial, frames, places, group):
    qkv_t, proj_t = attn_w
    up_t, down_t = mlp_w
    bias_three, up_b, bias_rows = biases
    rows = resid.shape[0]
    (first,) = rows_call(first_rows, rows, (resid,), (parts,), (BF,), False)
    first_all = jnp.concatenate([first, swap_core(first)], axis=0)
    qkv = row_major((nt_dot(first_all, qkv_t) + bias_three).astype(BF))
    width = qkv.shape[1] // 3
    mixed = attention_call(
        attention_kernel, (qkv,), width, spatial, frames, places, group, 4 * 512 * 256 * width
    )
    att_sum = nt_dot(mixed, proj_t)
    attended, middle, second = rows_call(
        middle_rows,
        rows,
        (att_sum, from_core_half(att_sum), resid),
        (parts, bias_rows),
        (F32, F32, BF),
        False,
    )
    seconds = gather_four(second)
    actives, slopes, branches = [], [], []
    for part in seconds:
        active, slope = gelu_both(nt_dot(part, up_t) + up_b)
        actives.append(active)
        slopes.append(slope)
        branches.append(nt_dot(active, down_t))
    near, far = branches
    branch, result = rows_call(
        result_rows,
        rows,
        (near, from_core_half(near), from_clip_rows(far), middle),
        (parts, bias_rows),
        (F32, BF),
        False,
    )
    kept = (resid, middle, first_all, qkv, mixed, attended, seconds, actives, slopes, branch)
    return (result, kept)


def block_backward(incoming, kept, parts, attn_w, mlp_w, ring, spatial, frames, places, group):
    resid, middle, first_all, qkv, mixed, attended, seconds, actives, slopes, branch = kept
    qkv_t, proj_t = attn_w
    up_t, down_t = mlp_w
    rows = incoming.shape[0]
    grad_branch, sums_open = rows_call(
        open_rows, rows, (incoming, branch), (parts,), (BF,), True
    )
    branches = gather_four(grad_branch)
    seconds_grad = []
    hiddens = []
    for part, slope in zip(branches, slopes):
        grad_hidden = (nn_dot(part, down_t) * slope.astype(F32)).astype(BF)
        hiddens.append(grad_hidden)
        seconds_grad.append(nn_dot(grad_hidden, up_t))
    bias_up = sum(jnp.sum(item, axis=0, dtype=F32) for item in hiddens)
    grad_down = sum(weight_grad(part, act) for part, act in zip(branches, actives)).astype(BF)
    grad_up = sum(weight_grad(item, part) for item, part in zip(hiddens, seconds)).astype(BF)
    scattered_mlp, mlp_marks = ring_scatter(ring, grad_up, grad_down)
    near, far = seconds_grad
    grad_middle, grad_att, sums_middle = rows_call(
        middle_back_rows,
        rows,
        (near, from_core_half(near), from_clip_rows(far), incoming, middle, attended),
        (parts,),
        (F32, BF),
        True,
    )
    grad_att_all = jnp.concatenate([grad_att, swap_core(grad_att)], axis=0)
    grad_mixed = row_major(nn_dot(grad_att_all, proj_t).astype(BF))
    grad_proj = row_major(weight_grad(grad_att_all, mixed).astype(BF))
    grad_three = attention_call(
        attention_back_kernel,
        (qkv, grad_mixed),
        qkv.shape[1],
        spatial,
        frames,
        places,
        group,
        10 * 512 * 256 * mixed.shape[1],
    )
    grad_first = nn_dot(grad_three, qkv_t)
    grad_resid, sums_first = rows_call(
        first_back_rows,
        rows,
        (grad_first, from_core_half(grad_first), grad_middle, resid),
        (parts,),
        (F32 if spatial else BF,),
        True,
    )
    if not spatial:
        grad_resid = to_frames(grad_resid, ring, frames, places)
    grad_qkv = weight_grad(grad_three, first_all).astype(BF)
    if not spatial:
        grad_qkv = after(grad_qkv, grad_resid)
    scattered_attn, attn_marks = ring_scatter(ring, grad_qkv, grad_proj)
    column_sums = jnp.sum(grad_three, axis=0, dtype=F32)
    mod_early = jnp.concatenate([sums_middle[2:3], sums_middle[0:2], sums_open[0:1]]).reshape(-1)
    mod_late = sums_first[0:2].reshape(-1)
    return (
        grad_resid,
        (mod_early, mod_late),
        (scattered_mlp, scattered_attn),
        (sums_open[1], sums_middle[3], bias_up, column_sums),
        (mlp_marks, attn_marks),
    )


def to_places(rows, ring, frames, places):
    cells = rows.reshape(frames, ring.size, places // ring.size, -1)
    moved = lax.all_to_all(cells, "seq", split_axis=1, concat_axis=0, tiled=True)
    return moved.reshape(frames * places, -1)


def to_frames(rows, ring, frames, places):
    cells = rows.reshape(ring.size * frames, 1, places // ring.size, -1)
    moved = lax.all_to_all(cells, "seq", split_axis=0, concat_axis=1, tiled=True)
    return moved.reshape(frames * places, -1)


def ringed(
    ring_size,
    tokens,
    condition,
    *rest,
):
    weights, cotangent = rest[:-1], rest[-1]
    layers = (weights[:10], weights[10:])
    clip = lax.axis_index("clip")
    core = lax.axis_index("fsdp")
    seat = lax.axis_index("seq")
    ring = Ring(ring_size)
    frames, places, width = tokens.shape[1:]
    group = places // ring_size
    cell = layers[0][6].shape[1] // 2

    attn_w, mlp_w = [None, None], [None, None]
    cell_rows = (cell, 2 * layers[0][8].shape[1])
    shapes = (
        (layers[0][2].shape[1], (2 * layers[0][4].shape[1], width // 2)),
        (cell_rows[0], (cell_rows[1], width)),
    )
    flags = jnp.stack([clip, core])
    attn_pieces = [AttentionPiece(layer[2], layer[4]) for layer in layers]
    feed_pieces = [FeedPiece(layer[6], layer[8]) for layer in layers]
    messages = make_messages(attn_pieces[:1], flags, [attn_pieces[0].weights])
    later = [feed_pieces[0], attn_pieces[1], feed_pieces[1]]
    later_weights = [item for piece in later for item in piece.weights]
    *later_weights, unused = lax.optimization_barrier((*later_weights, messages[0]))
    messages += make_messages(
        later, flags, [later_weights[:2], later_weights[2:4], later_weights[4:]]
    )
    attn_w[0], marks = ring_gather(ring, messages[0], *shapes[0])
    mlp_w[0], marks = ring_gather(ring, messages[1], *shapes[1], marks[-1])
    attn_w[1], marks = ring_gather(ring, messages[2], *shapes[0], marks[-1])
    mlp_w[1], marks = ring_gather(ring, messages[3], *shapes[1], marks[-1])
    cotangent = after(cotangent, marks[0])

    packed = jnp.concatenate(
        [layer[at].reshape(1, -1) for layer in layers for at in (1, 3, 5, 7, 9)], axis=1
    )
    both = order_two(clip, packed, swap_clip(packed), 0).astype(F32)
    vectors = []
    start = 0
    for layer in layers:
        row = []
        for at in (1, 3, 5, 7, 9):
            size = layer[at].shape[0]
            row.append(both[:, start : start + size].reshape(-1))
            start += size
        vectors.append(row)

    cond_in = condition.astype(F32)
    cond_act = jax.nn.silu(cond_in).astype(BF)
    acts = order_two(clip, cond_act, swap_clip(cond_act), 0)
    half = width // 2
    acts_half = pick(clip, acts[:, :half], acts[:, half:])
    mod_parts = jnp.stack([nn_dot(acts_half, layer[0]) for layer in layers], axis=1)
    mine = pick(clip, mod_parts[0], mod_parts[1])
    give = pick(clip, mod_parts[1], mod_parts[0])
    mod_cols = mine + swap_clip(give)
    columns = mod_cols.shape[1]
    slots = jnp.arange(2 * ring_size).reshape(1, -1, 1) == seat * 2 + core
    slots = jnp.where(slots, mod_cols[:, None, :], 0.0).reshape(2, 6 * width)
    mods = sum_seats(slots + swap_core(slots), ring_size)

    parts, biases = [], []
    for index in range(2):
        adab, qvb, projb, upb, downb = vectors[index]
        parts.append((mods[index] + adab).reshape(6, width))
        by_parity = qvb.reshape(2, -1, 2, HEAD)
        mine_qv = pick(core, by_parity[:, :, 0], by_parity[:, :, 1]).reshape(2, -1)
        three = jnp.concatenate([mine_qv[0], jnp.zeros_like(mine_qv[0]), mine_qv[1]])
        cells = upb.reshape(ring_size, 2, 2, cell)
        by_core = pick(core, cells[:, 0], cells[:, 1])
        mine_up = pick(clip, by_core[:, 0], by_core[:, 1]).reshape(-1)
        biases.append((three, mine_up, jnp.stack([projb, downb])))

    resid = tokens.reshape(-1, width)
    resid, kept_space = block_forward(
        resid, parts[0], attn_w[0], mlp_w[0], biases[0], True, frames, places, group
    )
    resid = to_places(resid, ring, frames, places)
    resid, kept_time = block_forward(
        resid, parts[1], attn_w[1], mlp_w[1], biases[1], False, frames, places, group
    )

    incoming = to_places(cotangent.reshape(-1, width), ring, frames, places)
    kept = (kept_space, kept_time)
    backs = [None, None]
    for index in (1, 0):
        back = block_backward(
            incoming,
            kept[index],
            parts[index],
            attn_w[index],
            mlp_w[index],
            ring,
            index == 0,
            frames,
            places,
            group,
        )
        backs[index] = back
        incoming = back[0]
    tokens_grad = incoming.reshape(tokens.shape)
    mlp_marks, last = backs[0][4]
    output = to_frames(resid, ring, frames, places).reshape(tokens.shape)

    def slots_of(index, mods, late):
        bias_down, bias_proj, bias_up, column_sums = backs[index][3]
        items = [stack_two(clip, mods, jnp.zeros_like(mods), 0).reshape(-1)]
        if not late:
            up_cells = bias_up.reshape(ring_size, cell)
            slots = stack_two(clip, up_cells, jnp.zeros_like(up_cells), 1)
            slots = stack_two(core, slots, jnp.zeros_like(slots), 1).reshape(-1)
            items += [bias_down, bias_proj, slots]
        if late:
            third = column_sums.shape[0] // 3
            qv = jnp.stack([column_sums[:third], column_sums[2 * third :]]).reshape(2, -1, HEAD)
            items.append(stack_two(core, qv, jnp.zeros_like(qv), 2).reshape(-1))
        return items

    def summed(items, marks=()):
        total = sum_all(jnp.concatenate(items), ring_size, marks)
        parts_of, start = [], 0
        for item in items:
            parts_of.append(total[start : start + item.shape[0]])
            start += item.shape[0]
        return parts_of

    time_items = slots_of(1, backs[1][1][0], False) + slots_of(1, backs[1][1][1], True)
    time_items = [after(item, mlp_marks[0]) for item in time_items]
    early = summed(time_items + slots_of(0, backs[0][1][0], False))
    late = summed(slots_of(0, backs[0][1][1], True), (last[0], last[0], last[1], last[1]))

    def joined_mod(early_part, late_part):
        return jnp.concatenate([late_part.reshape(2, -1), early_part.reshape(2, -1)], axis=1)

    totals = [None, None]
    totals[1] = (joined_mod(early[0], early[4]), early[1], early[2], early[3], early[5])
    totals[0] = (joined_mod(early[6], late[0]), early[7], early[8], early[9], late[1])

    def own_half(value):
        rows = value.reshape(2, -1)
        return pick(clip, rows[0], rows[1])

    held = [after(item, last[0]) for item in backs[1][2][1] + backs[1][2][0] + backs[0][2][0]]
    finished = make_gradients(
        [attn_pieces[1], feed_pieces[1], feed_pieces[0]],
        flags,
        [held[0:2], held[2:4], held[4:6]],
    )
    (closing,) = make_gradients([attn_pieces[0]], flags, [backs[0][2][1]])
    matrices = (closing + finished[2], finished[0] + finished[1])

    results = [None, None]
    grad_acts = jnp.zeros((2, half), F32)
    for index in (1, 0):
        grad_mods, bias_down, bias_proj, bias_up, bias_qv = totals[index]
        mod_low = grad_mods.astype(BF)
        mod_cols = lax.dynamic_slice_in_dim(mod_low, (seat * 2 + core) * columns, columns, 1)
        grad_acts = grad_acts + back_dot(mod_cols, layers[index][0])
        results[index] = (
            weight_grad(acts_half, mod_cols),
            own_half(jnp.sum(mod_low.astype(F32), axis=0)),
            matrices[index][0],
            own_half(bias_qv),
            matrices[index][1],
            own_half(bias_proj),
            matrices[index][2],
            own_half(bias_up),
            matrices[index][3],
            own_half(bias_down),
        )
    slots = stack_two(clip, grad_acts, jnp.zeros_like(grad_acts), 1).reshape(2, -1)
    total = sum_all(slots, ring_size)
    grad_act = pick(clip, total[0], total[1]).reshape(cond_in.shape)
    unused, silu_back = jax.vjp(jax.nn.silu, cond_in)
    condition_grad = silu_back(grad_act)[0]
    return (output, tokens_grad, condition_grad) + results[0] + results[1]


def solution(mesh):
    in_specs = (
        P("clip", "seq", "fsdp", None),
        P("clip", None),
        P("clip", ("seq", "fsdp")),
        P("clip"),
        P("clip", ("seq", "fsdp")),
        P("clip"),
        P("clip", ("seq", "fsdp")),
        P("clip"),
        P("clip", ("seq", "fsdp")),
        P("clip"),
        P("clip", ("seq", "fsdp")),
        P("clip"),
        P("clip", ("seq", "fsdp")),
        P("clip"),
        P("clip", ("seq", "fsdp")),
        P("clip"),
        P("clip", ("seq", "fsdp")),
        P("clip"),
        P("clip", ("seq", "fsdp")),
        P("clip"),
        P("clip", ("seq", "fsdp")),
        P("clip"),
        P("clip", "seq", "fsdp", None),
    )
    out_specs = (
        P("clip", "seq", "fsdp", None),
        P("clip", "seq", "fsdp", None),
        P("clip", None),
        P("clip", ("seq", "fsdp")),
        P("clip"),
        P("clip", ("seq", "fsdp")),
        P("clip"),
        P("clip", ("seq", "fsdp")),
        P("clip"),
        P("clip", ("seq", "fsdp")),
        P("clip"),
        P("clip", ("seq", "fsdp")),
        P("clip"),
        P("clip", ("seq", "fsdp")),
        P("clip"),
        P("clip", ("seq", "fsdp")),
        P("clip"),
        P("clip", ("seq", "fsdp")),
        P("clip"),
        P("clip", ("seq", "fsdp")),
        P("clip"),
        P("clip", ("seq", "fsdp")),
        P("clip"),
    )
    sizes = mesh.shape
    fits = (
        sizes["clip"] == 2
        and sizes["fsdp"] == 2
        and sizes["seq"] % 4 == 0
        and 16 * 3 % (2 * sizes["seq"]) == 0
        and 16 * 3 // (2 * sizes["seq"]) == 3
    )
    body = partial(ringed, sizes["seq"]) if fits else local
    return jax.shard_map(body, mesh=mesh, in_specs=in_specs, out_specs=out_specs, check_vma=False)
```
